32 devices in a mesh: dp: 8 (over y, x, core), group: 4 (over z).
Axes of the slice: x: 2, y: 2, z: 4, core: 2. Of those that a mesh axis runs over, the one named last changes fastest.
Arguments:
- tokens: bfloat16 [4096, 768], P(('dp', 'group')), may hold values from -6 to 6
- grad_out: bfloat16 [4096, 768], P(('dp', 'group')), may hold values from -6 to 6
- segment_ids: int32 [4096], P(('dp', 'group')), may hold values from 0 to 1023, as said below
- positions: int32 [4096], P(('dp', 'group')), may hold values from 0 to 511, as said below
- counts: int32 [32], P(('dp', 'group')), may hold values from 64 to 128, as said below
- master: float32 [7090176], P(('dp', 'group'))
- moment_one: float32 [7090176], P(('dp', 'group')), may hold values from -0.00021362305 to 0.00021362305
- moment_two: float32 [7090176], P(('dp', 'group')), may hold values from 2.8208045e-09 to 2.8208044e-08
Outputs:
- block_out: bfloat16 [4096, 768], P(('dp', 'group'))
- grad_in: bfloat16 [4096, 768], P(('dp', 'group'))
- weight_grads: float32 [7090176], P(('dp', 'group'))
- new_master: float32 [7090176], P(('dp', 'group'))
- new_moment_one: float32 [7090176], P(('dp', 'group'))
- new_moment_two: float32 [7090176], P(('dp', 'group'))
The draws below stay inside these ranges and needn't reach their ends.
Inputs may be any that keep to these rules, and one draw needn't show every extreme that they name: `counts`: in every batch of 4 devices at least one device uses all 128 slots; a device's used slots come first. The first batch uses all its slots; in the last batch the last device uses 128 // 2. `segment_ids`: used slots of a batch carry sequence numbers that never fall along the batch; the unused slot j of a batch carries 512 + j. A sequence may run over several devices of its batch; the first batch holds one sequence. `positions`: used slots carry their position counted from 0 within their sequence in slot order; unused slots carry 0.
All inputs are finite; a program needn't handle non-finite values.
Results may differ from the reference program's by a relative error of at most 0.019.
Values may be sent and summed in bfloat16 or wider, within the bound.
A program may use at most 192 MiB of HBM per device.

```python
import math
import jax
import jax.numpy as jnp
from jax import lax

D = 768
FF = 3072
HEAD = 64
ROT = 16
STEP = 3
TOK_DEV = 128
GROUP_SIZE = 4
BATCHES = 8
GROUP_ROWS = 512
TOKENS = 4096
NPAR = 7090176
DEVICES = 32


start_odds = 384


def param_layout_drawn(model_width, hidden):
    return [('weight_qkv', (model_width, 3 * model_width)), ('bias_qkv', (3 * model_width,)), ('weight_out', (model_width, model_width)), ('bias_out', (model_width,)), ('weight_up', (model_width, hidden)), ('bias_up', (hidden,)), ('weight_down', (hidden, model_width)), ('bias_down', (model_width,)), ('gain_attn', (model_width,)), ('shift_attn', (model_width,)), ('gain_mlp', (model_width,)), ('shift_mlp', (model_width,))]


def packing(key):
    base_key = jax.random.fold_in(key, 11)
    key_counts, key_full, key_coin = jax.random.split(base_key, 3)
    counts = jax.random.randint(key_counts, (BATCHES, GROUP_SIZE), TOK_DEV // 2, TOK_DEV + 1)
    full_device = jax.random.randint(key_full, (BATCHES,), 0, GROUP_SIZE)
    batch_index = jnp.arange(BATCHES)[:, None]
    device_index = jnp.arange(GROUP_SIZE)[None, :]
    full_device = jnp.where(jnp.arange(BATCHES) == BATCHES - 1, 0, full_device)
    counts = jnp.where(device_index == full_device[:, None], TOK_DEV, counts)
    counts = jnp.where(batch_index == 0, TOK_DEV, counts)
    counts = jnp.where((batch_index == BATCHES - 1) & (device_index == GROUP_SIZE - 1), TOK_DEV // 2, counts)
    counts = counts.astype(jnp.int32)
    valid_rows = (jnp.arange(TOK_DEV)[None, None, :] < counts[:, :, None]).reshape(BATCHES, GROUP_ROWS)
    valid_rank = jnp.cumsum(valid_rows.astype(jnp.int32), 1) - 1
    coin_draw = jax.random.randint(key_coin, (BATCHES, GROUP_ROWS), 0, start_odds)
    coin_start = (coin_draw == 0) & (batch_index > 0)
    starts = valid_rows & (coin_start | (valid_rank == 0))
    segment = jnp.cumsum(starts.astype(jnp.int32), 1) - 1
    slot_index = jnp.arange(GROUP_ROWS, dtype=jnp.int32)[None, :]
    segment = jnp.where(valid_rows, segment, GROUP_ROWS + slot_index)
    start_rank = lax.cummax(jnp.where(starts, valid_rank, -1), axis=1)
    position = jnp.where(valid_rows, valid_rank - start_rank, 0)
    return (counts.reshape(DEVICES), segment.reshape(TOKENS).astype(jnp.int32), position.reshape(TOKENS).astype(jnp.int32))


def draw_counts(key, part):
    return packing(key)[0]


def draw_segment_ids(key, part):
    return packing(key)[1]


def draw_positions(key, part):
    return packing(key)[2]


def draw_master(key, part):
    flat_index = jnp.arange(NPAR)
    raw_values = jax.random.normal(key, (NPAR,), jnp.float32)
    scale_table = {'weight_qkv': D ** (-0.5), 'bias_qkv': 0.1, 'weight_out': 3.0 * D ** (-0.5), 'bias_out': 0.1, 'weight_up': D ** (-0.5), 'bias_up': 0.1, 'weight_down': FF ** (-0.5), 'bias_down': 0.1, 'gain_attn': 0.1, 'shift_attn': 0.1, 'gain_mlp': 0.1, 'shift_mlp': 0.1}
    scale_vec = jnp.full((NPAR,), 0.02, jnp.float32)
    shift_vec = jnp.zeros((NPAR,), jnp.float32)
    offset = 0
    for entry_name, entry_shape in param_layout_drawn(D, FF):
        length = 1
        for extent in entry_shape:
            length = length * extent
        inside = (flat_index >= offset) & (flat_index < offset + length)
        scale_vec = jnp.where(inside, scale_table[entry_name], scale_vec)
        if entry_name in ('gain_attn', 'gain_mlp'):
            shift_vec = jnp.where(inside, 1.0, shift_vec)
        offset = offset + length
    return raw_values * scale_vec + shift_vec


def levels(key, shape, cuts, least, top_value):
    gain, own = 1.0, jax.random.fold_in(key, 6)
    for axis_at, parts in cuts:
        steps = jnp.exp(jax.random.uniform(jax.random.fold_in(own, axis_at), (parts,), jnp.float32, least / len(cuts), top_value / len(cuts)))
        gain = gain * jnp.repeat(steps, shape[axis_at] // parts).reshape([-1 if axis == axis_at else 1 for axis in range(len(shape))])
    return gain


def bell_draw(key, shape, width, limit, cuts=(), kind=jnp.bfloat16):
    loudness = levels(key, shape, cuts, -0.22, 0.18) if cuts else 1.0
    values = jax.random.normal(key, shape, jnp.float32) * width * loudness
    return jnp.minimum(jnp.maximum(values, -limit), limit).astype(kind)


def setup_inputs(seed: int = 0) -> dict:
    splits = jax.random.split(jax.random.key(seed), 9)
    return {
        "tokens": bell_draw(splits[0], (TOKENS, D), 1.0, 6.0, ((0, 32),)),
        "grad_out": bell_draw(splits[1], (TOKENS, D), 1.0, 6.0, ((0, 32),)),
        "segment_ids": draw_segment_ids(jax.random.fold_in(splits[8], 71), 0),
        "positions": draw_positions(jax.random.fold_in(splits[8], 71), 0),
        "counts": draw_counts(jax.random.fold_in(splits[8], 71), 0),
        "master": draw_master(jax.random.fold_in(splits[8], 71), 0),
        "moment_one": bell_draw(splits[6], (NPAR,), (0.1 / NPAR ** 0.5), 0.00021362305, ((0, 32),), jnp.float32),
        "moment_two": jnp.clip(jnp.exp(math.log(2.8208043900690427e-08) - 2.3025851 * jax.random.uniform(splits[7], (NPAR,), jnp.float32) ** levels(splits[7], (NPAR,), ((0, 32),), -0.2, 0.2)), 2.8208044788868847e-09, 2.8208043900690427e-08),
    }


BETA_ONE = 0.9
BETA_TWO = 0.95
LEARN_RATE = 0.01
DECAY_RATE = 0.1
ADAM_EPS = 1e-08
NORM_EPS = 1e-05
SCORE_SCALE = 0.125
MASKED = -1e+30

def param_layout(model_width, hidden):
    return [('weight_qkv', (model_width, 3 * model_width)), ('bias_qkv', (3 * model_width,)), ('weight_out', (model_width, model_width)), ('bias_out', (model_width,)), ('weight_up', (model_width, hidden)), ('bias_up', (hidden,)), ('weight_down', (hidden, model_width)), ('bias_down', (model_width,)), ('gain_attn', (model_width,)), ('shift_attn', (model_width,)), ('gain_mlp', (model_width,)), ('shift_mlp', (model_width,))]

def unpack_params(flat_params, model_width, hidden):
    result = {}
    offset = 0
    for entry_name, entry_shape in param_layout(model_width, hidden):
        length = 1
        for extent in entry_shape:
            length = length * extent
        result[entry_name] = flat_params[offset:offset + length].reshape(entry_shape)
        offset = offset + length
    return result

def pack_grads(grad_dict, model_width, hidden, total_len):
    pieces = []
    used_count = 0
    for entry_name, entry_shape in param_layout(model_width, hidden):
        flat_grad = grad_dict[entry_name].reshape(-1)
        pieces.append(flat_grad)
        used_count = used_count + flat_grad.shape[0]
    pieces.append(jnp.zeros((total_len - used_count,), jnp.float32))
    return jnp.concatenate(pieces)

def rotary_tables(pos_ids):
    half_rot = ROT // 2
    inverse_freq = 10000.0 ** (-jnp.arange(half_rot, dtype=jnp.float32) * 2.0 / ROT)
    angles = pos_ids.astype(jnp.float32)[:, None] * inverse_freq[None, :]
    return (jnp.cos(angles), jnp.sin(angles))

def rotate(values, cosine, sine_rows):
    half_rot = ROT // 2
    lower_part = values[..., :half_rot]
    upper_part = values[..., half_rot:ROT]
    cos_rows = cosine[:, None, :]
    sin_rows = sine_rows[:, None, :]
    return jnp.concatenate([lower_part * cos_rows - upper_part * sin_rows, upper_part * cos_rows + lower_part * sin_rows, values[..., ROT:]], -1)

def rotate_back(values, cosine, sine_rows):
    half_rot = ROT // 2
    lower_part = values[..., :half_rot]
    upper_part = values[..., half_rot:ROT]
    cos_rows = cosine[:, None, :]
    sin_rows = sine_rows[:, None, :]
    return jnp.concatenate([lower_part * cos_rows + upper_part * sin_rows, upper_part * cos_rows - lower_part * sin_rows, values[..., ROT:]], -1)

def layer_stats(block_in):
    centred = block_in - lax.optimization_barrier(jnp.mean(block_in, -1, keepdims=True))
    inv_std = lax.rsqrt(lax.optimization_barrier(jnp.mean(centred * centred, -1, keepdims=True)) + NORM_EPS)
    return (centred * inv_std, inv_std)

def norm_backward(grad_normed, normed, inv_std):
    return inv_std * (grad_normed - lax.optimization_barrier(jnp.mean(grad_normed, -1, keepdims=True)) - normed * lax.optimization_barrier(jnp.mean(grad_normed * normed, -1, keepdims=True)))

def gelu_slope(up_pre):
    return 0.5 * (1.0 + lax.erf(up_pre * 0.7071067811865476)) + up_pre * jnp.exp(-0.5 * up_pre * up_pre) * 0.3989422804014327

def group_pass(block_tokens, cotangent, seg_ids, pos_ids, valid_rows, params):
    rows_here = block_tokens.shape[0]
    head_count = D // HEAD
    block_in = block_tokens.astype(jnp.float32)
    normed, inv_std = layer_stats(block_in)
    gain_attn = params['gain_attn'].astype(jnp.float32)
    gain_mlp = params['gain_mlp'].astype(jnp.float32)
    attn_in = (normed * gain_attn + params['shift_attn'].astype(jnp.float32)).astype(jnp.bfloat16)
    mlp_in = (normed * gain_mlp + params['shift_mlp'].astype(jnp.float32)).astype(jnp.bfloat16)
    qkv_pre = (jnp.dot(attn_in, params['weight_qkv'], preferred_element_type=jnp.float32) + params['bias_qkv'].astype(jnp.float32)).reshape(rows_here, 3, head_count, HEAD)
    cosine, sine_rows = rotary_tables(pos_ids)
    queries = rotate(qkv_pre[:, 0], cosine, sine_rows).astype(jnp.bfloat16)
    keys_rot = rotate(qkv_pre[:, 1], cosine, sine_rows).astype(jnp.bfloat16)
    values = qkv_pre[:, 2].astype(jnp.bfloat16)
    slot_index = jnp.arange(rows_here)
    allowed = (seg_ids[:, None] == seg_ids[None, :]) & (slot_index[None, :] <= slot_index[:, None])
    scores = jnp.einsum('qhd,khd->hqk', queries.astype(jnp.float32), keys_rot.astype(jnp.float32)) * SCORE_SCALE
    scores = jnp.where(allowed[None], scores, MASKED)
    row_max = lax.optimization_barrier(jnp.max(scores, -1, keepdims=True))
    log_total = row_max + jnp.log(lax.optimization_barrier(jnp.sum(jnp.exp(scores - row_max), -1, keepdims=True)))
    attn_probs = jnp.exp(scores - log_total)
    probs_low = attn_probs.astype(jnp.bfloat16)
    context = jnp.einsum('hqk,khd->qhd', probs_low.astype(jnp.float32), values.astype(jnp.float32)).astype(jnp.bfloat16)
    context_flat = context.reshape(rows_here, D)
    attn_out = jnp.dot(context_flat, params['weight_out'], preferred_element_type=jnp.float32) + params['bias_out'].astype(jnp.float32)
    up_pre = jnp.dot(mlp_in, params['weight_up'], preferred_element_type=jnp.float32) + params['bias_up'].astype(jnp.float32)
    up_act = jax.nn.gelu(up_pre, approximate=False).astype(jnp.bfloat16)
    mlp_out = jnp.dot(up_act, params['weight_down'], preferred_element_type=jnp.float32) + params['bias_down'].astype(jnp.float32)
    block_out = (block_in + attn_out + mlp_out).astype(jnp.bfloat16)
    grad_rows = cotangent.astype(jnp.float32) * valid_rows[:, None]
    grad_low = grad_rows.astype(jnp.bfloat16)
    bias_grad = lax.optimization_barrier(jnp.sum(grad_rows, 0))
    grad_dict = {}
    grad_dict['weight_down'] = jnp.dot(up_act.T, grad_low, preferred_element_type=jnp.float32)
    grad_dict['bias_down'] = bias_grad
    grad_dict['weight_out'] = jnp.dot(context_flat.T, grad_low, preferred_element_type=jnp.float32)
    grad_dict['bias_out'] = bias_grad
    grad_act = jnp.dot(grad_low, params['weight_down'].T, preferred_element_type=jnp.float32)
    grad_pre = (grad_act * gelu_slope(up_pre)).astype(jnp.bfloat16)
    grad_dict['weight_up'] = jnp.dot(mlp_in.T, grad_pre, preferred_element_type=jnp.float32)
    grad_dict['bias_up'] = lax.optimization_barrier(jnp.sum(grad_pre.astype(jnp.float32), 0))
    grad_mlp_in = jnp.dot(grad_pre, params['weight_up'].T, preferred_element_type=jnp.float32)
    grad_context = jnp.dot(grad_low, params['weight_out'].T, preferred_element_type=jnp.float32).astype(jnp.bfloat16)
    grad_context = grad_context.reshape(rows_here, head_count, HEAD)
    row_delta = jnp.einsum('qhd,qhd->hq', grad_context.astype(jnp.float32), context.astype(jnp.float32))
    grad_probs = jnp.einsum('qhd,khd->hqk', grad_context.astype(jnp.float32), values.astype(jnp.float32))
    grad_scores = (attn_probs * (grad_probs - row_delta[..., None]) * SCORE_SCALE).astype(jnp.bfloat16)
    grad_queries = jnp.einsum('hqk,khd->qhd', grad_scores.astype(jnp.float32), keys_rot.astype(jnp.float32))
    grad_keys = jnp.einsum('hqk,qhd->khd', grad_scores.astype(jnp.float32), queries.astype(jnp.float32))
    grad_values = jnp.einsum('hqk,qhd->khd', probs_low.astype(jnp.float32), grad_context.astype(jnp.float32))
    grad_qkv = jnp.stack([rotate_back(grad_queries, cosine, sine_rows), rotate_back(grad_keys, cosine, sine_rows), grad_values], 1).reshape(rows_here, 3 * D).astype(jnp.bfloat16)
    grad_dict['weight_qkv'] = jnp.dot(attn_in.T, grad_qkv, preferred_element_type=jnp.float32)
    grad_dict['bias_qkv'] = lax.optimization_barrier(jnp.sum(grad_qkv.astype(jnp.float32), 0))
    grad_attn_in = jnp.dot(grad_qkv, params['weight_qkv'].T, preferred_element_type=jnp.float32)
    grad_dict['gain_attn'] = lax.optimization_barrier(jnp.sum(grad_attn_in * normed, 0))
    grad_dict['shift_attn'] = lax.optimization_barrier(jnp.sum(grad_attn_in, 0))
    grad_dict['gain_mlp'] = lax.optimization_barrier(jnp.sum(grad_mlp_in * normed, 0))
    grad_dict['shift_mlp'] = lax.optimization_barrier(jnp.sum(grad_mlp_in, 0))
    grad_normed = grad_attn_in * gain_attn + grad_mlp_in * gain_mlp
    grad_in = (grad_rows + norm_backward(grad_normed, normed, inv_std)).astype(jnp.bfloat16)
    return (block_out, grad_in, grad_dict)

def reference(tokens, grad_out, segment_ids, positions, counts, master, moment_one, moment_two):
    params = unpack_params(master.astype(jnp.bfloat16), D, FF)
    valid_rows = (jnp.arange(TOK_DEV)[None, :] < counts[:, None]).astype(jnp.float32).reshape(BATCHES, GROUP_ROWS)
    inputs_all = (tokens.reshape(BATCHES, GROUP_ROWS, D), grad_out.reshape(BATCHES, GROUP_ROWS, D), segment_ids.reshape(BATCHES, GROUP_ROWS), positions.reshape(BATCHES, GROUP_ROWS), valid_rows)
    zero_grads = {}
    for entry_name, entry_shape in param_layout(D, FF):
        zero_grads[entry_name] = jnp.zeros(entry_shape, jnp.float32)

    def scan_group(totals, group_inputs):
        block_tokens, cotangent, seg_ids, pos_ids, valid_here = group_inputs
        block_out, grad_in, grad_dict = group_pass(block_tokens, cotangent, seg_ids, pos_ids, valid_here, params)
        summed = jax.tree.map(lambda running, addend: running + addend, totals, grad_dict)
        return (summed, (block_out, grad_in))
    totals, (outs_all, grads_all) = lax.scan(scan_group, zero_grads, inputs_all)
    flat_grads = pack_grads(totals, D, FF, NPAR)
    square_sum = jnp.sum(flat_grads * flat_grads)
    grad_scale = 1.0 / (jnp.sqrt(square_sum) + 1e-06)
    scaled = flat_grads * grad_scale
    new_one = BETA_ONE * moment_one + (1.0 - BETA_ONE) * scaled
    new_two = BETA_TWO * moment_two + (1.0 - BETA_TWO) * scaled * scaled
    correct_one = 1.0 - BETA_ONE ** STEP
    correct_two = 1.0 - BETA_TWO ** STEP
    new_master = master - LEARN_RATE * (new_one / correct_one / (jnp.sqrt(new_two / correct_two) + ADAM_EPS) + DECAY_RATE * master)
    return (outs_all.reshape(TOKENS, D), grads_all.reshape(TOKENS, D), flat_grads, new_master, new_one, new_two)
```

```python
import functools

import jax
import jax.numpy as jnp
import numpy as np
from jax import lax
from jax.sharding import PartitionSpec as P

FF = 3072
HEAD = 64
ROT = 16
STEP = 3


BETA_ONE = 0.9
BETA_TWO = 0.95
LEARN_RATE = 0.01
DECAY_RATE = 0.1
ADAM_EPS = 1e-08
NORM_EPS = 1e-05
SCORE_SCALE = 0.125
MASKED = -1e30


def param_layout(model_width, hidden):
    return [
        ("weight_qkv", (model_width, 3 * model_width)),
        ("bias_qkv", (3 * model_width,)),
        ("weight_out", (model_width, model_width)),
        ("bias_out", (model_width,)),
        ("weight_up", (model_width, hidden)),
        ("bias_up", (hidden,)),
        ("weight_down", (hidden, model_width)),
        ("bias_down", (model_width,)),
        ("gain_attn", (model_width,)),
        ("shift_attn", (model_width,)),
        ("gain_mlp", (model_width,)),
        ("shift_mlp", (model_width,)),
    ]


def unpack_params(flat_params, model_width, hidden):
    result = {}
    offset = 0
    for entry_name, entry_shape in param_layout(model_width, hidden):
        length = 1
        for extent in entry_shape:
            length = length * extent
        result[entry_name] = flat_params[offset : offset + length].reshape(entry_shape)
        offset = offset + length
    return result


def pack_grads(grad_dict, model_width, hidden, total_len):
    pieces = []
    used_count = 0
    for entry_name, entry_shape in param_layout(model_width, hidden):
        flat_grad = grad_dict[entry_name].reshape(-1)
        pieces.append(flat_grad)
        used_count = used_count + flat_grad.shape[0]
    pieces.append(jnp.zeros((total_len - used_count,), jnp.float32))
    return jnp.concatenate(pieces)


def rotary_tables(pos_ids):
    half_rot = ROT // 2
    inverse_freq = 10000.0 ** (-jnp.arange(half_rot, dtype=jnp.float32) * 2.0 / ROT)
    angles = pos_ids.astype(jnp.float32)[:, None] * inverse_freq[None, :]
    return (jnp.cos(angles), jnp.sin(angles))


def rotate(values, cosine, sine_rows):
    half_rot = ROT // 2
    lower_part = values[..., :half_rot]
    upper_part = values[..., half_rot:ROT]
    cos_rows = cosine[:, None, :]
    sin_rows = sine_rows[:, None, :]
    return jnp.concatenate(
        [
            lower_part * cos_rows - upper_part * sin_rows,
            upper_part * cos_rows + lower_part * sin_rows,
            values[..., ROT:],
        ],
        -1,
    )


def rotate_back(values, cosine, sine_rows):
    half_rot = ROT // 2
    lower_part = values[..., :half_rot]
    upper_part = values[..., half_rot:ROT]
    cos_rows = cosine[:, None, :]
    sin_rows = sine_rows[:, None, :]
    return jnp.concatenate(
        [
            lower_part * cos_rows + upper_part * sin_rows,
            upper_part * cos_rows - lower_part * sin_rows,
            values[..., ROT:],
        ],
        -1,
    )


def layer_stats(block_in):
    centred = block_in - jnp.mean(block_in, -1, keepdims=True)
    inv_std = lax.rsqrt(jnp.mean(centred * centred, -1, keepdims=True) + NORM_EPS)
    return (centred * inv_std, inv_std)


def norm_backward(grad_normed, normed, inv_std):
    return inv_std * (
        grad_normed
        - jnp.mean(grad_normed, -1, keepdims=True)
        - normed * jnp.mean(grad_normed * normed, -1, keepdims=True)
    )


def gelu_slope(up_pre):
    return (
        0.5 * (1.0 + lax.erf(up_pre * 0.7071067811865476))
        + up_pre * jnp.exp(-0.5 * up_pre * up_pre) * 0.3989422804014327
    )


def masked_scores(query_part, key_part, query_seg, key_seg, query_slot, key_slot):
    scores = (
        jnp.einsum("qhd,khd->hqk", query_part, key_part, preferred_element_type=jnp.float32)
        * SCORE_SCALE
    )
    allowed = (query_seg[:, None] == key_seg[None, :]) & (key_slot[None, :] <= query_slot[:, None])
    return (jnp.where(allowed[None], scores, MASKED), allowed)


def score_grads(scores, allowed, log_total, row_delta, grad_context, value_part):
    attn_probs = jnp.where(allowed[None], jnp.exp(scores - log_total[..., None]), 0.0)
    grad_probs = jnp.einsum(
        "qhd,khd->hqk", grad_context, value_part, preferred_element_type=jnp.float32
    )
    grad_scores = (attn_probs * (grad_probs - row_delta[..., None]) * SCORE_SCALE).astype(
        jnp.bfloat16
    )
    return (attn_probs.astype(jnp.bfloat16), grad_scores)


def on_device_gathered(tokens, grad_out, segment_ids, positions, counts, master, moment_one, moment_two):
    local_rows = tokens.shape[0]
    model_width = tokens.shape[1]
    head_count = model_width // HEAD
    local_master = master.astype(jnp.bfloat16)
    sectioned = lax.all_gather(local_master.reshape(1, 1, -1), "group", axis=1, tiled=True)
    sectioned = lax.all_gather(sectioned, "dp", axis=0, tiled=True)
    flat_params = sectioned.reshape(-1)
    params = unpack_params(flat_params, model_width, FF)
    block_in = tokens.astype(jnp.float32)
    normed, inv_std = layer_stats(block_in)
    gain_attn = params["gain_attn"].astype(jnp.float32)
    gain_mlp = params["gain_mlp"].astype(jnp.float32)
    attn_in = (normed * gain_attn + params["shift_attn"].astype(jnp.float32)).astype(jnp.bfloat16)
    mlp_in = (normed * gain_mlp + params["shift_mlp"].astype(jnp.float32)).astype(jnp.bfloat16)
    qkv_pre = (
        jnp.dot(attn_in, params["weight_qkv"], preferred_element_type=jnp.float32)
        + params["bias_qkv"].astype(jnp.float32)
    ).reshape(local_rows, 3, head_count, HEAD)
    cosine, sine_rows = rotary_tables(positions)
    queries = rotate(qkv_pre[:, 0], cosine, sine_rows).astype(jnp.bfloat16)
    keys_own = rotate(qkv_pre[:, 1], cosine, sine_rows).astype(jnp.bfloat16)
    values_own = qkv_pre[:, 2].astype(jnp.bfloat16)
    key_vals = jnp.stack(
        [keys_own.reshape(local_rows, model_width), values_own.reshape(local_rows, model_width)], 1
    )
    query_slot = lax.axis_index("group") * local_rows + jnp.arange(local_rows, dtype=jnp.int32)

    def split_keys(piece_kv):
        count_keys = piece_kv.shape[0]
        return (
            piece_kv[:, 0].reshape(count_keys, head_count, HEAD),
            piece_kv[:, 1].reshape(count_keys, head_count, HEAD),
        )

    run_max = jnp.full((head_count, local_rows), MASKED, jnp.float32)
    piece_kv = lax.all_gather(key_vals, "group", axis=0, tiled=True)
    piece_seg = lax.all_gather(segment_ids, "group", axis=0, tiled=True)
    piece_keys, piece_values = split_keys(piece_kv)
    key_slot = jnp.arange(piece_seg.shape[0], dtype=jnp.int32)
    scores, allowed = masked_scores(
        queries, piece_keys, segment_ids, piece_seg, query_slot, key_slot
    )
    new_max = jnp.maximum(run_max, jnp.max(scores, -1))
    weights = jnp.where(allowed[None], jnp.exp(scores - new_max[..., None]), 0.0)
    run_sum = jnp.sum(weights, -1)
    run_acc = jnp.einsum(
        "hqk,khd->hqd",
        weights.astype(jnp.bfloat16),
        piece_values,
        preferred_element_type=jnp.float32,
    )
    run_max, run_sum, run_acc = (new_max, run_sum, run_acc)
    log_total = run_max + jnp.log(run_sum)
    context = jnp.transpose(run_acc / run_sum[..., None], (1, 0, 2)).astype(jnp.bfloat16)
    context_flat = context.reshape(local_rows, model_width)
    attn_out = jnp.dot(
        context_flat, params["weight_out"], preferred_element_type=jnp.float32
    ) + params["bias_out"].astype(jnp.float32)
    up_pre = jnp.dot(mlp_in, params["weight_up"], preferred_element_type=jnp.float32) + params[
        "bias_up"
    ].astype(jnp.float32)
    up_act = jax.nn.gelu(up_pre, approximate=False).astype(jnp.bfloat16)
    mlp_out = jnp.dot(up_act, params["weight_down"], preferred_element_type=jnp.float32) + params[
        "bias_down"
    ].astype(jnp.float32)
    block_out = (block_in + attn_out + mlp_out).astype(jnp.bfloat16)
    valid_rows = (jnp.arange(local_rows) < counts[0]).astype(jnp.float32)
    grad_rows = grad_out.astype(jnp.float32) * valid_rows[:, None]
    grad_low = grad_rows.astype(jnp.bfloat16)
    bias_grad = jnp.sum(grad_rows, 0)
    grad_dict = {}
    grad_dict["weight_down"] = jnp.dot(up_act.T, grad_low, preferred_element_type=jnp.float32)
    grad_dict["bias_down"] = bias_grad
    grad_dict["weight_out"] = jnp.dot(context_flat.T, grad_low, preferred_element_type=jnp.float32)
    grad_dict["bias_out"] = bias_grad
    grad_act = jnp.dot(grad_low, params["weight_down"].T, preferred_element_type=jnp.float32)
    grad_pre = (grad_act * gelu_slope(up_pre)).astype(jnp.bfloat16)
    grad_dict["weight_up"] = jnp.dot(mlp_in.T, grad_pre, preferred_element_type=jnp.float32)
    grad_dict["bias_up"] = jnp.sum(grad_pre.astype(jnp.float32), 0)
    grad_mlp_in = jnp.dot(grad_pre, params["weight_up"].T, preferred_element_type=jnp.float32)
    grad_context = jnp.dot(
        grad_low, params["weight_out"].T, preferred_element_type=jnp.float32
    ).astype(jnp.bfloat16)
    grad_context = grad_context.reshape(local_rows, head_count, HEAD)
    row_delta = jnp.einsum(
        "qhd,qhd->hq", grad_context.astype(jnp.float32), context.astype(jnp.float32)
    )
    piece_kv = lax.all_gather(key_vals, "group", axis=0, tiled=True)
    piece_seg = lax.all_gather(segment_ids, "group", axis=0, tiled=True)
    piece_keys, piece_values = split_keys(piece_kv)
    count_keys = piece_seg.shape[0]
    key_slot = jnp.arange(count_keys, dtype=jnp.int32)
    scores, allowed = masked_scores(
        queries, piece_keys, segment_ids, piece_seg, query_slot, key_slot
    )
    probs_low, grad_scores = score_grads(
        scores, allowed, log_total, row_delta, grad_context, piece_values
    )
    grad_queries = jnp.einsum(
        "hqk,khd->qhd", grad_scores, piece_keys, preferred_element_type=jnp.float32
    )
    part_keys = jnp.einsum("hqk,qhd->khd", grad_scores, queries, preferred_element_type=jnp.float32)
    part_values = jnp.einsum(
        "hqk,qhd->khd", probs_low, grad_context, preferred_element_type=jnp.float32
    )
    addition = jnp.stack(
        [part_keys.reshape(count_keys, model_width), part_values.reshape(count_keys, model_width)],
        1,
    )
    grad_kv = addition
    grad_queries, batch_kv = (grad_queries, grad_kv)
    grad_kv = lax.psum_scatter(
        batch_kv.astype(jnp.bfloat16), "group", scatter_dimension=0, tiled=True
    ).astype(jnp.float32)
    grad_keys = grad_kv[:, 0].reshape(local_rows, head_count, HEAD)
    grad_values = grad_kv[:, 1].reshape(local_rows, head_count, HEAD)
    grad_qkv = (
        jnp.stack(
            [
                rotate_back(grad_queries, cosine, sine_rows),
                rotate_back(grad_keys, cosine, sine_rows),
                grad_values,
            ],
            1,
        )
        .reshape(local_rows, 3 * model_width)
        .astype(jnp.bfloat16)
    )
    grad_dict["weight_qkv"] = jnp.dot(attn_in.T, grad_qkv, preferred_element_type=jnp.float32)
    grad_dict["bias_qkv"] = jnp.sum(grad_qkv.astype(jnp.float32), 0)
    grad_attn_in = jnp.dot(grad_qkv, params["weight_qkv"].T, preferred_element_type=jnp.float32)
    grad_dict["gain_attn"] = jnp.sum(grad_attn_in * normed, 0)
    grad_dict["shift_attn"] = jnp.sum(grad_attn_in, 0)
    grad_dict["gain_mlp"] = jnp.sum(grad_mlp_in * normed, 0)
    grad_dict["shift_mlp"] = jnp.sum(grad_mlp_in, 0)
    grad_normed = grad_attn_in * gain_attn + grad_mlp_in * gain_mlp
    grad_in = (grad_rows + norm_backward(grad_normed, normed, inv_std)).astype(jnp.bfloat16)
    dp_count = lax.axis_size("dp")
    group_count = lax.axis_size("group")
    partial_value = pack_grads(grad_dict, model_width, FF, master.shape[0] * dp_count * group_count)
    sectioned_grad = lax.psum_scatter(
        partial_value.reshape(dp_count, group_count, -1).astype(jnp.bfloat16),
        "group",
        scatter_dimension=1,
        tiled=True,
    )
    grad_shard = (
        lax.psum_scatter(sectioned_grad, "dp", scatter_dimension=0, tiled=True)
        .astype(jnp.float32)
        .reshape(-1)
    )
    square_sum = lax.psum(jnp.sum(grad_shard * grad_shard), ("dp", "group"))
    grad_scale = 1.0 / (jnp.sqrt(square_sum) + 1e-06)
    scaled = grad_shard * grad_scale
    new_one = BETA_ONE * moment_one + (1.0 - BETA_ONE) * scaled
    new_two = BETA_TWO * moment_two + (1.0 - BETA_TWO) * scaled * scaled
    correct_one = 1.0 - BETA_ONE**STEP
    correct_two = 1.0 - BETA_TWO**STEP
    new_master = master - LEARN_RATE * (
        new_one / correct_one / (jnp.sqrt(new_two / correct_two) + ADAM_EPS) + DECAY_RATE * master
    )
    return (block_out, grad_in, grad_shard, new_master, new_one, new_two)


def part_rows(model_width, hidden, dp_count, group_count):
    up_rows = model_width // dp_count
    down_rows = hidden // group_count // dp_count
    out_rows = model_width // group_count // dp_count
    vec_rows = -(-8 // dp_count)
    vec_rows = -(-vec_rows // 8) * 8
    return up_rows, down_rows, up_rows, out_rows, vec_rows


@functools.lru_cache(None)
def exchange_tables(model_width, hidden, dp_count, group_count, shard_len):
    width = model_width
    unit = width // group_count
    unit_count = shard_len // unit
    per_line = group_count
    offsets, at = {}, 0
    for entry_name, entry_shape in param_layout(width, hidden):
        offsets[entry_name] = at // width
        at += int(np.prod(entry_shape))
    up_lines = hidden // width
    devices = dp_count * group_count
    sections = part_rows(width, hidden, dp_count, group_count)
    up_rows, down_rows, qkv_rows, out_rows, vec_rows = sections
    total_rows = sum(sections)
    vectors = [
        ("bias_qkv", 3),
        ("bias_up", up_lines),
        ("bias_out", 0),
        ("bias_down", 0),
        ("gain_attn", 0),
        ("shift_attn", 0),
        ("gain_mlp", 0),
        ("shift_mlp", 0),
    ]
    want = np.full((devices, total_rows, per_line), -1, np.int64)
    for d in range(dp_count):
        for g in range(group_count):
            here = want[d * group_count + g]
            row = 0
            for i in range(up_rows):
                r = i * dp_count + d
                for j in range(up_lines):
                    here[row, j] = (offsets["weight_up"] + up_lines * r + j) * per_line + g
                row += 1
            for i in range(down_rows):
                k = i * dp_count + d
                h = width * (k // unit) + unit * g + k % unit
                for j in range(per_line):
                    here[row, j] = (offsets["weight_down"] + h) * per_line + j
                row += 1
            for i in range(qkv_rows):
                r = i * dp_count + d
                for j in range(3):
                    here[row, j] = (3 * r + j) * per_line + g
                row += 1
            for i in range(out_rows):
                h = unit * g + i * dp_count + d
                for j in range(per_line):
                    here[row, j] = (offsets["weight_out"] + h) * per_line + j
                row += 1
            for v, (entry_name, split) in enumerate(vectors):
                if v % dp_count != d:
                    continue
                at_row = row + v // dp_count
                for j in range(split or per_line):
                    base = offsets[entry_name] + (j if split else 0)
                    here[at_row, j] = base * per_line + (g if split else j)
    counts = np.zeros((devices, devices), np.int64)
    sends = [[[] for _ in range(devices)] for _ in range(devices)]
    places = []
    for dest in range(devices):
        for row in range(total_rows):
            for j in range(per_line):
                u = want[dest, row, j]
                if u < 0:
                    continue
                owner = u // unit_count
                slot = counts[owner, dest]
                sends[owner][dest].append(u % unit_count)
                places.append((dest, row, j, owner, slot))
                counts[owner, dest] += 1
    most = -(-int(counts.max()) // 16) * 16
    send = np.full((devices, devices, most), -1, np.int32)
    for owner in range(devices):
        for dest in range(devices):
            units = sends[owner][dest]
            send[owner, dest, : len(units)] = units
    recv = np.full((devices, per_line, total_rows), -1, np.int32)
    for dest, row, j, owner, slot in places:
        recv[dest, j, row] = owner * most + slot
    return send.reshape(devices, devices * most), recv


def spread(size, step):
    each = size // step
    column = np.arange(size)
    natural = (column % each) * step + column // each
    rows = jnp.arange(size, dtype=jnp.int32)
    return (rows[:, None] == jnp.asarray(natural, jnp.int32)[None, :]).astype(jnp.bfloat16)


def pick(lhs, rhs):
    return jnp.dot(lhs, rhs, preferred_element_type=jnp.float32).astype(jnp.bfloat16)


def rotary_wide(pos_ids, width):
    half_rot = ROT // 2
    lane = jnp.arange(width, dtype=jnp.int32) % HEAD
    step = (lane % half_rot).astype(jnp.float32)
    inverse_freq = 10000.0 ** (-step * 2.0 / ROT)
    angles = pos_ids[:, None] * inverse_freq[None, :]
    cosine = jnp.where(lane[None] < ROT, jnp.cos(angles), 1.0)
    sine = jnp.sin(angles)
    low = jnp.where(lane[None] < half_rot, sine, 0.0)
    high = jnp.where((lane[None] >= half_rot) & (lane[None] < ROT), sine, 0.0)
    return cosine, low, high


def turn(values, tables, sign):
    cosine, low, high = tables
    half_rot = ROT // 2
    ahead = jnp.roll(values, -half_rot, 1)
    behind = jnp.roll(values, half_rot, 1)
    return values * cosine + sign * (behind * high - ahead * low)


def on_device_split(tokens, grad_out, segment_ids, positions, counts, master, moment_one, moment_two):
    f32, bf16 = jnp.float32, jnp.bfloat16
    dp_count, group_count = lax.axis_size("dp"), lax.axis_size("group")
    both = ("dp", "group")
    local_rows, width = tokens.shape
    rows = local_rows * group_count
    unit = width // group_count
    hidden = FF // group_count
    heads = unit // HEAD
    shard_len = master.shape[0]
    unit_count = shard_len // unit
    me = lax.axis_index("dp") * group_count + lax.axis_index("group")
    send, recv = exchange_tables(width, FF, dp_count, group_count, shard_len)
    sections = part_rows(width, FF, dp_count, group_count)
    starts = np.cumsum((0,) + sections)
    total_rows = int(starts[-1])
    slots = send.shape[1]

    def mm(lhs, rhs):
        return jnp.dot(lhs, rhs, preferred_element_type=f32)

    def mm_t(lhs, rhs):
        return lax.dot_general(lhs, rhs, (((1,), (1,)), ((), ())), preferred_element_type=f32)

    def t_mm(lhs, rhs):
        return lax.dot_general(lhs, rhs, (((0,), (0,)), ((), ())), preferred_element_type=f32)

    send_row = lax.dynamic_index_in_dim(jnp.asarray(send), me, 0, keepdims=False)
    recv_row = lax.dynamic_index_in_dim(jnp.asarray(recv), me, 0, keepdims=False)
    send_hot = (send_row[:, None] == jnp.arange(unit_count, dtype=jnp.int32)[None, :]).astype(bf16)
    recv_hot = (recv_row[:, :, None] == jnp.arange(slots, dtype=jnp.int32)[None, None, :]).astype(bf16)
    own_units = master.astype(bf16).reshape(unit_count, unit)
    moved = lax.all_to_all(pick(send_hot, own_units), both, 0, 0, tiled=True)
    part = jnp.concatenate([pick(recv_hot[j], moved) for j in range(group_count)], 1)
    whole = lax.all_gather(part, "dp", axis=0, tiled=False)

    def section(index):
        return whole[:, starts[index] : starts[index + 1]].reshape(-1, width)

    weight_up, weight_down, weight_qkv, weight_out = (section(i) for i in range(4))
    weight_qkv = weight_qkv[:, : 3 * unit]
    vec_all = jnp.stack(
        [whole[v % dp_count, int(starts[4]) + v // dp_count] for v in range(8)]
    )
    wide = spread(width, dp_count)
    narrow = spread(unit, dp_count)
    hidden_wide = spread(hidden, dp_count)
    bias_qkv = vec_all[0].astype(f32)[: 3 * unit]
    weight_up = pick(weight_up, hidden_wide)
    vec_turned = pick(vec_all, wide).astype(f32)
    bias_up = pick(vec_all[1:2, :hidden], hidden_wide).astype(f32)[0]
    bias_rest = vec_all[2].astype(f32) + vec_all[3].astype(f32)
    gain_attn, shift_attn, gain_mlp, shift_mlp = (vec_turned[4 + i] for i in range(4))

    valid_rows = jnp.arange(local_rows) < counts[0]
    grad_own = jnp.where(valid_rows[:, None], grad_out, jnp.zeros_like(grad_out))
    base = 256
    digits = [segment_ids // base, segment_ids % base, positions // base, positions % base]
    digits = jnp.stack(digits, 1).astype(bf16)
    digits = jnp.pad(digits, ((0, 0), (0, 124)))
    batch = lax.all_gather(
        jnp.concatenate([tokens, grad_own, digits], 1), "group", axis=0, tiled=True
    )
    grad_low = batch[:, width : 2 * width]
    digits = batch[:, 2 * width :].astype(f32)
    segment = digits[:, 0] * base + digits[:, 1]
    place = digits[:, 2] * base + digits[:, 3]
    block_in = mm(batch[:, :width], wide)
    normed, inv_std = layer_stats(block_in)
    attn_in = (normed * gain_attn + shift_attn).astype(bf16)
    mlp_in = (normed * gain_mlp + shift_mlp).astype(bf16)

    qkv_pre = mm(attn_in, weight_qkv) + bias_qkv
    tables = rotary_wide(place, unit)
    queries = turn(qkv_pre[:, :unit], tables, 1.0).astype(bf16)
    keys = turn(qkv_pre[:, unit : 2 * unit], tables, 1.0).astype(bf16)
    values = qkv_pre[:, 2 * unit :].astype(bf16)
    slot = jnp.arange(rows, dtype=jnp.int32)
    allowed = (segment[:, None] == segment[None, :]) & (slot[None, :] <= slot[:, None])

    grad_context = pick_t(grad_low, weight_out)
    grad_context = mm_t(grad_context, narrow).astype(bf16)
    context_parts, grad_q, grad_k, grad_v = [], [], [], []
    for h in range(heads):
        cut = slice(h * HEAD, (h + 1) * HEAD)
        q, k, v, gc = queries[:, cut], keys[:, cut], values[:, cut], grad_context[:, cut]
        scores = jnp.where(allowed, mm_t(q, k) * SCORE_SCALE, MASKED)
        top = jnp.max(scores, -1, keepdims=True)
        weights = jnp.exp(scores - top)
        probs = weights / jnp.sum(weights, -1, keepdims=True)
        probs_low = probs.astype(bf16)
        context = mm(probs_low, v).astype(bf16)
        context_parts.append(context)
        row_delta = jnp.sum(gc.astype(f32) * context.astype(f32), -1, keepdims=True)
        grad_scores = (probs * (mm_t(gc, v) - row_delta) * SCORE_SCALE).astype(bf16)
        grad_q.append(mm(grad_scores, k))
        grad_k.append(t_mm(grad_scores, q))
        grad_v.append(t_mm(probs_low, gc))
    context = pick(jnp.concatenate(context_parts, 1), narrow)
    grad_qkv = jnp.concatenate(
        [
            turn(jnp.concatenate(grad_q, 1), tables, -1.0),
            turn(jnp.concatenate(grad_k, 1), tables, -1.0),
        ]
        + grad_v,
        1,
    ).astype(bf16)

    up_pre = mm(mlp_in, weight_up) + bias_up
    up_act = jax.nn.gelu(up_pre, approximate=False).astype(bf16)
    out_part = mm(context, weight_out) + mm(up_act, weight_down)
    grad_pre = (mm_t(grad_low, weight_down) * gelu_slope(up_pre)).astype(bf16)
    grad_mlp_in = mm_t(grad_pre, weight_up)
    grad_attn_in = mm_t(grad_qkv, weight_qkv)

    def pad_wide(value):
        return jnp.pad(value, ((0, 0), (0, width - value.shape[1])))

    def parts_of(value):
        return value.reshape(dp_count, -1, width)

    natural_vecs = jnp.stack(
        [
            jnp.sum(grad_attn_in * normed, 0),
            jnp.sum(grad_attn_in, 0),
            jnp.sum(grad_mlp_in * normed, 0),
            jnp.sum(grad_mlp_in, 0),
        ]
    ).astype(bf16)
    natural_vecs = mm_t(natural_vecs, wide).astype(bf16)
    bias_grad = jnp.sum(grad_own.astype(f32), 0).astype(bf16)[None]
    bias_up_grad = mm_t(jnp.sum(grad_pre.astype(f32), 0).astype(bf16)[None], hidden_wide).astype(bf16)
    bias_qkv_grad = jnp.sum(grad_qkv.astype(f32), 0).astype(bf16)[None]
    vec_grads = jnp.concatenate(
        [pad_wide(bias_qkv_grad), pad_wide(bias_up_grad), bias_grad, bias_grad, natural_vecs], 0
    )
    vec_rows = sections[4]
    vec_grads = jnp.pad(vec_grads, ((0, dp_count * vec_rows - 8), (0, 0)))
    vec_grads = jnp.transpose(vec_grads.reshape(vec_rows, dp_count, width), (1, 0, 2))
    packed = jnp.concatenate(
        [
            parts_of(mm_t(t_mm(mlp_in, grad_pre).astype(bf16), hidden_wide).astype(bf16)),
            parts_of(t_mm(up_act, grad_low).astype(bf16)),
            parts_of(pad_wide(t_mm(attn_in, grad_qkv).astype(bf16))),
            parts_of(t_mm(context, grad_low).astype(bf16)),
            vec_grads,
        ],
        1,
    )
    summed = reduce_parts(packed)
    returned = sum(
        t_mm(recv_hot[j], summed[:, j * unit : (j + 1) * unit]) for j in range(group_count)
    ).astype(bf16)
    returned = lax.all_to_all(returned, both, 0, 0, tiled=True)
    grad_shard = t_mm(send_hot, returned).reshape(-1)

    grad_normed = (grad_attn_in * gain_attn + grad_mlp_in * gain_mlp).astype(bf16)
    grad_normed = mm_t(grad_normed, wide).astype(bf16)
    swapped = lax.all_to_all(
        jnp.concatenate([out_part.astype(bf16), grad_normed], 1), "group", 0, 0, tiled=True
    )
    own = jnp.sum(swapped.astype(f32).reshape(group_count, local_rows, 2 * width), 0)
    tokens_own = tokens.astype(f32)
    block_out = (tokens_own + own[:, :width] + bias_rest).astype(bf16)
    own_normed, own_inv = layer_stats(tokens_own)
    grad_in = (grad_own.astype(f32) + norm_backward(own[:, width:], own_normed, own_inv)).astype(bf16)

    square_sum = lax.psum(jnp.sum(grad_shard * grad_shard), both)
    return (block_out, grad_in) + update(grad_shard, square_sum, master, moment_one, moment_two)


def pick_t(lhs, rhs):
    return lax.dot_general(
        lhs, rhs, (((1,), (1,)), ((), ())), preferred_element_type=jnp.float32
    ).astype(jnp.bfloat16)


def reduce_parts(packed):
    return lax.psum_scatter(packed, "dp", scatter_dimension=0, tiled=False)


def update(grad_shard, square_sum, master, moment_one, moment_two):
    grad_scale = 1.0 / (jnp.sqrt(square_sum) + 1e-06)
    scaled = grad_shard * grad_scale
    new_one = BETA_ONE * moment_one + (1.0 - BETA_ONE) * scaled
    new_two = BETA_TWO * moment_two + (1.0 - BETA_TWO) * scaled * scaled
    correct_one = 1.0 - BETA_ONE**STEP
    correct_two = 1.0 - BETA_TWO**STEP
    new_master = master - LEARN_RATE * (
        new_one / correct_one / (jnp.sqrt(new_two / correct_two) + ADAM_EPS) + DECAY_RATE * master
    )
    return (grad_shard, new_master, new_one, new_two)


def on_device(tokens, grad_out, segment_ids, positions, counts, master, moment_one, moment_two):
    dp_count, group_count = lax.axis_size("dp"), lax.axis_size("group")
    width = tokens.shape[1]
    splits = (
        (width // HEAD) % group_count == 0
        and FF == width * group_count
        and (width // group_count) % dp_count == 0
        and master.shape[0] % (width // group_count) == 0
    )
    body = on_device_split if splits else on_device_gathered
    return body(tokens, grad_out, segment_ids, positions, counts, master, moment_one, moment_two)


def solution(mesh):
    placed = (
        P(("dp", "group"), None),
        P(("dp", "group"), None),
        P(("dp", "group")),
        P(("dp", "group")),
        P(("dp", "group")),
        P(("dp", "group")),
        P(("dp", "group")),
        P(("dp", "group")),
    )
    return jax.shard_map(
        on_device,
        mesh=mesh,
        in_specs=placed,
        out_specs=(
            P(("dp", "group"), None),
            P(("dp", "group"), None),
            P(("dp", "group")),
            P(("dp", "group")),
            P(("dp", "group")),
            P(("dp", "group")),
        ),
        check_vma=False,
    )
```

```python
import functools

import jax
import jax.numpy as jnp
import numpy as np
from jax import lax
from jax.sharding import PartitionSpec as P

FF = 3072
HEAD = 64
ROT = 16
STEP = 3


BETA_ONE = 0.9
BETA_TWO = 0.95
LEARN_RATE = 0.01
DECAY_RATE = 0.1
ADAM_EPS = 1e-08
NORM_EPS = 1e-05
SCORE_SCALE = 0.125
MASKED = -1e30
EXTRA_LINES = 3


def param_layout(model_width, hidden):
    return [
        ("weight_qkv", (model_width, 3 * model_width)),
        ("bias_qkv", (3 * model_width,)),
        ("weight_out", (model_width, model_width)),
        ("bias_out", (model_width,)),
        ("weight_up", (model_width, hidden)),
        ("bias_up", (hidden,)),
        ("weight_down", (hidden, model_width)),
        ("bias_down", (model_width,)),
        ("gain_attn", (model_width,)),
        ("shift_attn", (model_width,)),
        ("gain_mlp", (model_width,)),
        ("shift_mlp", (model_width,)),
    ]


def unpack_params(flat_params, model_width, hidden):
    result = {}
    offset = 0
    for entry_name, entry_shape in param_layout(model_width, hidden):
        length = 1
        for extent in entry_shape:
            length = length * extent
        result[entry_name] = flat_params[offset : offset + length].reshape(entry_shape)
        offset = offset + length
    return result


def pack_grads(grad_dict, model_width, hidden, total_len):
    pieces = []
    used_count = 0
    for entry_name, entry_shape in param_layout(model_width, hidden):
        flat_grad = grad_dict[entry_name].reshape(-1)
        pieces.append(flat_grad)
        used_count = used_count + flat_grad.shape[0]
    pieces.append(jnp.zeros((total_len - used_count,), jnp.float32))
    return jnp.concatenate(pieces)


def rotary_tables(pos_ids):
    half_rot = ROT // 2
    inverse_freq = 10000.0 ** (-jnp.arange(half_rot, dtype=jnp.float32) * 2.0 / ROT)
    angles = pos_ids.astype(jnp.float32)[:, None] * inverse_freq[None, :]
    return (jnp.cos(angles), jnp.sin(angles))


def rotate(values, cosine, sine_rows):
    half_rot = ROT // 2
    lower_part = values[..., :half_rot]
    upper_part = values[..., half_rot:ROT]
    cos_rows = cosine[:, None, :]
    sin_rows = sine_rows[:, None, :]
    return jnp.concatenate(
        [
            lower_part * cos_rows - upper_part * sin_rows,
            upper_part * cos_rows + lower_part * sin_rows,
            values[..., ROT:],
        ],
        -1,
    )


def rotate_back(values, cosine, sine_rows):
    half_rot = ROT // 2
    lower_part = values[..., :half_rot]
    upper_part = values[..., half_rot:ROT]
    cos_rows = cosine[:, None, :]
    sin_rows = sine_rows[:, None, :]
    return jnp.concatenate(
        [
            lower_part * cos_rows + upper_part * sin_rows,
            upper_part * cos_rows - lower_part * sin_rows,
            values[..., ROT:],
        ],
        -1,
    )


def layer_stats(block_in):
    centred = block_in - jnp.mean(block_in, -1, keepdims=True)
    inv_std = lax.rsqrt(jnp.mean(centred * centred, -1, keepdims=True) + NORM_EPS)
    return (centred * inv_std, inv_std)


def norm_backward(grad_normed, normed, inv_std):
    return inv_std * (
        grad_normed
        - jnp.mean(grad_normed, -1, keepdims=True)
        - normed * jnp.mean(grad_normed * normed, -1, keepdims=True)
    )


def gelu_slope(up_pre):
    return (
        0.5 * (1.0 + lax.erf(up_pre * 0.7071067811865476))
        + up_pre * jnp.exp(-0.5 * up_pre * up_pre) * 0.3989422804014327
    )


def masked_scores(query_part, key_part, query_seg, key_seg, query_slot, key_slot):
    scores = (
        jnp.einsum("qhd,khd->hqk", query_part, key_part, preferred_element_type=jnp.float32)
        * SCORE_SCALE
    )
    allowed = (query_seg[:, None] == key_seg[None, :]) & (key_slot[None, :] <= query_slot[:, None])
    return (jnp.where(allowed[None], scores, MASKED), allowed)


def score_grads(scores, allowed, log_total, row_delta, grad_context, value_part):
    attn_probs = jnp.where(allowed[None], jnp.exp(scores - log_total[..., None]), 0.0)
    grad_probs = jnp.einsum(
        "qhd,khd->hqk", grad_context, value_part, preferred_element_type=jnp.float32
    )
    grad_scores = (attn_probs * (grad_probs - row_delta[..., None]) * SCORE_SCALE).astype(
        jnp.bfloat16
    )
    return (attn_probs.astype(jnp.bfloat16), grad_scores)


def on_device_gathered(tokens, grad_out, segment_ids, positions, counts, master, moment_one, moment_two):
    local_rows = tokens.shape[0]
    model_width = tokens.shape[1]
    head_count = model_width // HEAD
    local_master = master.astype(jnp.bfloat16)
    sectioned = lax.all_gather(local_master.reshape(1, 1, -1), "group", axis=1, tiled=True)
    sectioned = lax.all_gather(sectioned, "dp", axis=0, tiled=True)
    flat_params = sectioned.reshape(-1)
    params = unpack_params(flat_params, model_width, FF)
    block_in = tokens.astype(jnp.float32)
    normed, inv_std = layer_stats(block_in)
    gain_attn = params["gain_attn"].astype(jnp.float32)
    gain_mlp = params["gain_mlp"].astype(jnp.float32)
    attn_in = (normed * gain_attn + params["shift_attn"].astype(jnp.float32)).astype(jnp.bfloat16)
    mlp_in = (normed * gain_mlp + params["shift_mlp"].astype(jnp.float32)).astype(jnp.bfloat16)
    qkv_pre = (
        jnp.dot(attn_in, params["weight_qkv"], preferred_element_type=jnp.float32)
        + params["bias_qkv"].astype(jnp.float32)
    ).reshape(local_rows, 3, head_count, HEAD)
    cosine, sine_rows = rotary_tables(positions)
    queries = rotate(qkv_pre[:, 0], cosine, sine_rows).astype(jnp.bfloat16)
    keys_own = rotate(qkv_pre[:, 1], cosine, sine_rows).astype(jnp.bfloat16)
    values_own = qkv_pre[:, 2].astype(jnp.bfloat16)
    key_vals = jnp.stack(
        [keys_own.reshape(local_rows, model_width), values_own.reshape(local_rows, model_width)], 1
    )
    query_slot = lax.axis_index("group") * local_rows + jnp.arange(local_rows, dtype=jnp.int32)

    def split_keys(piece_kv):
        count_keys = piece_kv.shape[0]
        return (
            piece_kv[:, 0].reshape(count_keys, head_count, HEAD),
            piece_kv[:, 1].reshape(count_keys, head_count, HEAD),
        )

    run_max = jnp.full((head_count, local_rows), MASKED, jnp.float32)
    piece_kv = lax.all_gather(key_vals, "group", axis=0, tiled=True)
    piece_seg = lax.all_gather(segment_ids, "group", axis=0, tiled=True)
    piece_keys, piece_values = split_keys(piece_kv)
    key_slot = jnp.arange(piece_seg.shape[0], dtype=jnp.int32)
    scores, allowed = masked_scores(
        queries, piece_keys, segment_ids, piece_seg, query_slot, key_slot
    )
    new_max = jnp.maximum(run_max, jnp.max(scores, -1))
    weights = jnp.where(allowed[None], jnp.exp(scores - new_max[..., None]), 0.0)
    run_sum = jnp.sum(weights, -1)
    run_acc = jnp.einsum(
        "hqk,khd->hqd",
        weights.astype(jnp.bfloat16),
        piece_values,
        preferred_element_type=jnp.float32,
    )
    run_max, run_sum, run_acc = (new_max, run_sum, run_acc)
    log_total = run_max + jnp.log(run_sum)
    context = jnp.transpose(run_acc / run_sum[..., None], (1, 0, 2)).astype(jnp.bfloat16)
    context_flat = context.reshape(local_rows, model_width)
    attn_out = jnp.dot(
        context_flat, params["weight_out"], preferred_element_type=jnp.float32
    ) + params["bias_out"].astype(jnp.float32)
    up_pre = jnp.dot(mlp_in, params["weight_up"], preferred_element_type=jnp.float32) + params[
        "bias_up"
    ].astype(jnp.float32)
    up_act = jax.nn.gelu(up_pre, approximate=False).astype(jnp.bfloat16)
    mlp_out = jnp.dot(up_act, params["weight_down"], preferred_element_type=jnp.float32) + params[
        "bias_down"
    ].astype(jnp.float32)
    block_out = (block_in + attn_out + mlp_out).astype(jnp.bfloat16)
    valid_rows = (jnp.arange(local_rows) < counts[0]).astype(jnp.float32)
    grad_rows = grad_out.astype(jnp.float32) * valid_rows[:, None]
    grad_low = grad_rows.astype(jnp.bfloat16)
    bias_grad = jnp.sum(grad_rows, 0)
    grad_dict = {}
    grad_dict["weight_down"] = jnp.dot(up_act.T, grad_low, preferred_element_type=jnp.float32)
    grad_dict["bias_down"] = bias_grad
    grad_dict["weight_out"] = jnp.dot(context_flat.T, grad_low, preferred_element_type=jnp.float32)
    grad_dict["bias_out"] = bias_grad
    grad_act = jnp.dot(grad_low, params["weight_down"].T, preferred_element_type=jnp.float32)
    grad_pre = (grad_act * gelu_slope(up_pre)).astype(jnp.bfloat16)
    grad_dict["weight_up"] = jnp.dot(mlp_in.T, grad_pre, preferred_element_type=jnp.float32)
    grad_dict["bias_up"] = jnp.sum(grad_pre.astype(jnp.float32), 0)
    grad_mlp_in = jnp.dot(grad_pre, params["weight_up"].T, preferred_element_type=jnp.float32)
    grad_context = jnp.dot(
        grad_low, params["weight_out"].T, preferred_element_type=jnp.float32
    ).astype(jnp.bfloat16)
    grad_context = grad_context.reshape(local_rows, head_count, HEAD)
    row_delta = jnp.einsum(
        "qhd,qhd->hq", grad_context.astype(jnp.float32), context.astype(jnp.float32)
    )
    piece_kv = lax.all_gather(key_vals, "group", axis=0, tiled=True)
    piece_seg = lax.all_gather(segment_ids, "group", axis=0, tiled=True)
    piece_keys, piece_values = split_keys(piece_kv)
    count_keys = piece_seg.shape[0]
    key_slot = jnp.arange(count_keys, dtype=jnp.int32)
    scores, allowed = masked_scores(
        queries, piece_keys, segment_ids, piece_seg, query_slot, key_slot
    )
    probs_low, grad_scores = score_grads(
        scores, allowed, log_total, row_delta, grad_context, piece_values
    )
    grad_queries = jnp.einsum(
        "hqk,khd->qhd", grad_scores, piece_keys, preferred_element_type=jnp.float32
    )
    part_keys = jnp.einsum("hqk,qhd->khd", grad_scores, queries, preferred_element_type=jnp.float32)
    part_values = jnp.einsum(
        "hqk,qhd->khd", probs_low, grad_context, preferred_element_type=jnp.float32
    )
    addition = jnp.stack(
        [part_keys.reshape(count_keys, model_width), part_values.reshape(count_keys, model_width)],
        1,
    )
    grad_kv = addition
    grad_queries, batch_kv = (grad_queries, grad_kv)
    grad_kv = lax.psum_scatter(
        batch_kv.astype(jnp.bfloat16), "group", scatter_dimension=0, tiled=True
    ).astype(jnp.float32)
    grad_keys = grad_kv[:, 0].reshape(local_rows, head_count, HEAD)
    grad_values = grad_kv[:, 1].reshape(local_rows, head_count, HEAD)
    grad_qkv = (
        jnp.stack(
            [
                rotate_back(grad_queries, cosine, sine_rows),
                rotate_back(grad_keys, cosine, sine_rows),
                grad_values,
            ],
            1,
        )
        .reshape(local_rows, 3 * model_width)
        .astype(jnp.bfloat16)
    )
    grad_dict["weight_qkv"] = jnp.dot(attn_in.T, grad_qkv, preferred_element_type=jnp.float32)
    grad_dict["bias_qkv"] = jnp.sum(grad_qkv.astype(jnp.float32), 0)
    grad_attn_in = jnp.dot(grad_qkv, params["weight_qkv"].T, preferred_element_type=jnp.float32)
    grad_dict["gain_attn"] = jnp.sum(grad_attn_in * normed, 0)
    grad_dict["shift_attn"] = jnp.sum(grad_attn_in, 0)
    grad_dict["gain_mlp"] = jnp.sum(grad_mlp_in * normed, 0)
    grad_dict["shift_mlp"] = jnp.sum(grad_mlp_in, 0)
    grad_normed = grad_attn_in * gain_attn + grad_mlp_in * gain_mlp
    grad_in = (grad_rows + norm_backward(grad_normed, normed, inv_std)).astype(jnp.bfloat16)
    dp_count = lax.axis_size("dp")
    group_count = lax.axis_size("group")
    partial_value = pack_grads(grad_dict, model_width, FF, master.shape[0] * dp_count * group_count)
    sectioned_grad = lax.psum_scatter(
        partial_value.reshape(dp_count, group_count, -1).astype(jnp.bfloat16),
        "group",
        scatter_dimension=1,
        tiled=True,
    )
    grad_shard = (
        lax.psum_scatter(sectioned_grad, "dp", scatter_dimension=0, tiled=True)
        .astype(jnp.float32)
        .reshape(-1)
    )
    square_sum = lax.psum(jnp.sum(grad_shard * grad_shard), ("dp", "group"))
    grad_scale = 1.0 / (jnp.sqrt(square_sum) + 1e-06)
    scaled = grad_shard * grad_scale
    new_one = BETA_ONE * moment_one + (1.0 - BETA_ONE) * scaled
    new_two = BETA_TWO * moment_two + (1.0 - BETA_TWO) * scaled * scaled
    correct_one = 1.0 - BETA_ONE**STEP
    correct_two = 1.0 - BETA_TWO**STEP
    new_master = master - LEARN_RATE * (
        new_one / correct_one / (jnp.sqrt(new_two / correct_two) + ADAM_EPS) + DECAY_RATE * master
    )
    return (block_out, grad_in, grad_shard, new_master, new_one, new_two)


def part_rows(model_width, hidden, dp_count, group_count):
    up_rows = model_width // dp_count
    down_rows = hidden // group_count // dp_count
    out_rows = model_width // group_count // dp_count
    vec_rows = -(-8 // dp_count)
    vec_rows = -(-vec_rows // 8) * 8
    return up_rows, down_rows, vec_rows, up_rows, out_rows


@functools.lru_cache(None)
def exchange_tables(model_width, hidden, dp_count, group_count, shard_len):
    width = model_width
    unit = width // group_count
    unit_count = shard_len // unit
    per_line = group_count
    offsets, at = {}, 0
    for entry_name, entry_shape in param_layout(width, hidden):
        offsets[entry_name] = at // width
        at += int(np.prod(entry_shape))
    up_lines = hidden // width
    devices = dp_count * group_count
    sections = part_rows(width, hidden, dp_count, group_count)
    up_rows, down_rows, vec_rows, qkv_rows, out_rows = sections
    total_rows = sum(sections)
    vectors = [
        ("bias_qkv", 3),
        ("bias_up", up_lines),
        ("bias_out", 0),
        ("bias_down", 0),
        ("gain_attn", 0),
        ("shift_attn", 0),
        ("gain_mlp", 0),
        ("shift_mlp", 0),
    ]
    want = np.full((devices, total_rows, per_line), -1, np.int64)
    for d in range(dp_count):
        for g in range(group_count):
            here = want[d * group_count + g]
            row = 0
            for i in range(up_rows):
                r = i * dp_count + d
                for j in range(up_lines):
                    here[row, j] = (offsets["weight_up"] + up_lines * r + j) * per_line + g
                row += 1
            for i in range(down_rows):
                k = i * dp_count + d
                h = width * (k // unit) + unit * g + k % unit
                for j in range(per_line):
                    here[row, j] = (offsets["weight_down"] + h) * per_line + j
                row += 1
            for v, (entry_name, split) in enumerate(vectors):
                if v % dp_count != d:
                    continue
                at_row = row + v // dp_count
                for j in range(split or per_line):
                    base = offsets[entry_name] + (j if split else 0)
                    here[at_row, j] = base * per_line + (g if split else j)
            row += vec_rows
            for i in range(qkv_rows):
                r = i * dp_count + d
                for j in range(3):
                    here[row, j] = (3 * r + j) * per_line + g
                row += 1
            for i in range(out_rows):
                h = unit * g + i * dp_count + d
                for j in range(per_line):
                    here[row, j] = (offsets["weight_out"] + h) * per_line + j
                row += 1
    counts = np.zeros((devices, devices), np.int64)
    sends = [[[] for _ in range(devices)] for _ in range(devices)]
    places = []
    for dest in range(devices):
        for row in range(total_rows):
            for j in range(per_line):
                u = want[dest, row, j]
                if u < 0:
                    continue
                owner = u // unit_count
                slot = counts[owner, dest]
                sends[owner][dest].append(u % unit_count)
                places.append((dest, row, j, owner, slot))
                counts[owner, dest] += 1
    lines = -(-((int(counts.max()) + 1) // 2 + EXTRA_LINES) // 8) * 8
    send = np.full((devices, 2, devices, lines), -1, np.int32)
    for owner in range(devices):
        for dest in range(devices):
            units = sends[owner][dest]
            for slot, u in enumerate(units):
                send[owner, slot % 2, dest, slot // 2] = u
    recv = np.full((devices, per_line, total_rows), -1, np.int32)
    for dest, row, j, owner, slot in places:
        recv[dest, j, row] = (slot % 2 * devices + owner) * lines + slot // 2
    return send.reshape(devices, 2, devices * lines), recv, lines


def spread(size, step):
    each = size // step
    column = np.arange(size)
    natural = (column % each) * step + column // each
    rows = jnp.arange(size, dtype=jnp.int32)
    return (rows[:, None] == jnp.asarray(natural, jnp.int32)[None, :]).astype(jnp.bfloat16)


def pick(lhs, rhs):
    return jnp.dot(lhs, rhs, preferred_element_type=jnp.float32).astype(jnp.bfloat16)


def rotary_wide(pos_ids, width):
    half_rot = ROT // 2
    lane = jnp.arange(width, dtype=jnp.int32) % HEAD
    step = (lane % half_rot).astype(jnp.float32)
    inverse_freq = 10000.0 ** (-step * 2.0 / ROT)
    angles = pos_ids[:, None] * inverse_freq[None, :]
    cosine = jnp.where(lane[None] < ROT, jnp.cos(angles), 1.0)
    sine = jnp.sin(angles)
    low = jnp.where(lane[None] < half_rot, sine, 0.0)
    high = jnp.where((lane[None] >= half_rot) & (lane[None] < ROT), sine, 0.0)
    return cosine, low, high


def turn(values, tables, sign):
    cosine, low, high = tables
    half_rot = ROT // 2
    ahead = jnp.roll(values, -half_rot, 1)
    behind = jnp.roll(values, half_rot, 1)
    return values * cosine + sign * (behind * high - ahead * low)


def on_device_split(tokens, grad_out, segment_ids, positions, counts, master, moment_one, moment_two):
    f32, bf16 = jnp.float32, jnp.bfloat16
    dp_count, group_count = lax.axis_size("dp"), lax.axis_size("group")
    both = ("dp", "group")
    local_rows, width = tokens.shape
    rows = local_rows * group_count
    unit = width // group_count
    hidden = FF // group_count
    heads = unit // HEAD
    shard_len = master.shape[0]
    unit_count = shard_len // unit
    me = lax.axis_index("dp") * group_count + lax.axis_index("group")
    send, recv, lines = exchange_tables(width, FF, dp_count, group_count, shard_len)
    sections = part_rows(width, FF, dp_count, group_count)
    starts = np.cumsum((0,) + sections)
    total_rows = int(starts[-1])
    side = send.shape[2]
    slots = 2 * side
    mlp_rows = int(starts[2])
    first_rows = int(starts[3])

    def mm(lhs, rhs):
        return jnp.dot(lhs, rhs, preferred_element_type=f32)

    def mm_t(lhs, rhs):
        return lax.dot_general(lhs, rhs, (((1,), (1,)), ((), ())), preferred_element_type=f32)

    def t_mm(lhs, rhs):
        return lax.dot_general(lhs, rhs, (((0,), (0,)), ((), ())), preferred_element_type=f32)

    send_row = lax.dynamic_index_in_dim(jnp.asarray(send), me, 0, keepdims=False)
    recv_row = lax.dynamic_index_in_dim(jnp.asarray(recv), me, 0, keepdims=False)
    send_hot = (send_row[:, :, None] == jnp.arange(unit_count, dtype=jnp.int32)).astype(bf16)
    recv_hot = (recv_row[:, :, None] == jnp.arange(slots, dtype=jnp.int32)).astype(bf16)
    own_units = master.astype(bf16).reshape(unit_count, unit)
    leaving = jnp.concatenate([pick(send_hot[half], own_units) for half in range(2)], 1)
    moved = lax.all_to_all(leaving, both, 0, 0, tiled=True)
    moved = [moved[:, :unit], moved[:, unit:]]

    def gather_rows(low, high):
        pieces = []
        for j in range(group_count):
            hot = recv_hot[j, low:high]
            pieces.append((mm(hot[:, :side], moved[0]) + mm(hot[:, side:], moved[1])).astype(bf16))
        return lax.all_gather(jnp.concatenate(pieces, 1), "dp", axis=0, tiled=False)

    whole_mlp = gather_rows(0, first_rows)
    whole_attn = gather_rows(first_rows, total_rows)
    weight_up = whole_mlp[:, : starts[1]].reshape(-1, width)
    weight_down = whole_mlp[:, starts[1] : mlp_rows].reshape(-1, width)
    vec_all = whole_mlp[:8, mlp_rows]
    wide = spread(width, dp_count)
    narrow = spread(unit, dp_count)
    hidden_wide = spread(hidden, dp_count)
    bias_qkv = vec_all[0].astype(f32)[: 3 * unit]
    weight_up = pick(weight_up, hidden_wide)
    vec_turned = pick(vec_all, wide).astype(f32)
    bias_up = pick(vec_all[1:2, :hidden], hidden_wide).astype(f32)[0]
    bias_rest = vec_all[2].astype(f32) + vec_all[3].astype(f32)
    gain_attn, shift_attn, gain_mlp, shift_mlp = (vec_turned[4 + i] for i in range(4))

    valid_rows = jnp.arange(local_rows) < counts[0]
    grad_own = jnp.where(valid_rows[:, None], grad_out, jnp.zeros_like(grad_out))
    base = 256
    digits = [segment_ids // base, segment_ids % base, positions // base, positions % base]
    digits = jnp.stack(digits, 1).astype(bf16)
    digits = jnp.pad(digits, ((0, 0), (0, 124)))
    batch = lax.all_gather(
        jnp.concatenate([tokens, grad_own, digits], 1), "group", axis=0, tiled=True
    )
    grad_low = batch[:, width : 2 * width]
    digits = batch[:, 2 * width :].astype(f32)
    segment = digits[:, 0] * base + digits[:, 1]
    place = digits[:, 2] * base + digits[:, 3]
    block_in = mm(batch[:, :width], wide)
    normed, inv_std = layer_stats(block_in)
    attn_in = (normed * gain_attn + shift_attn).astype(bf16)
    mlp_in = (normed * gain_mlp + shift_mlp).astype(bf16)

    def parts_of(value):
        return value.reshape(dp_count, -1, width)

    up_pre = mm(mlp_in, weight_up) + bias_up
    up_act = jax.nn.gelu(up_pre, approximate=False).astype(bf16)
    mlp_out = mm(up_act, weight_down)
    grad_pre = (mm_t(grad_low, weight_down) * gelu_slope(up_pre)).astype(bf16)
    grad_mlp_in = mm_t(grad_pre, weight_up)
    packed_mlp = jnp.concatenate(
        [
            parts_of(mm_t(t_mm(mlp_in, grad_pre).astype(bf16), hidden_wide).astype(bf16)),
            parts_of(t_mm(up_act, grad_low).astype(bf16)),
        ],
        1,
    )
    whole_attn, packed_mlp = lax.optimization_barrier((whole_attn, packed_mlp))
    summed_mlp = reduce_parts(packed_mlp)
    weight_qkv = whole_attn[:, : sections[3]].reshape(-1, width)[:, : 3 * unit]
    weight_out = whole_attn[:, sections[3] :].reshape(-1, width)

    qkv_pre = mm(attn_in, weight_qkv) + bias_qkv
    tables = rotary_wide(place, unit)
    queries = turn(qkv_pre[:, :unit], tables, 1.0).astype(bf16)
    keys = turn(qkv_pre[:, unit : 2 * unit], tables, 1.0).astype(bf16)
    values = qkv_pre[:, 2 * unit :].astype(bf16)
    slot = jnp.arange(rows, dtype=jnp.int32)
    allowed = (segment[:, None] == segment[None, :]) & (slot[None, :] <= slot[:, None])

    grad_context = pick_t(grad_low, weight_out)
    grad_context = mm_t(grad_context, narrow).astype(bf16)
    context_parts, grad_q, grad_k, grad_v = [], [], [], []
    for h in range(heads):
        cut = slice(h * HEAD, (h + 1) * HEAD)
        q, k, v, gc = queries[:, cut], keys[:, cut], values[:, cut], grad_context[:, cut]
        scores = jnp.where(allowed, mm_t(q, k) * SCORE_SCALE, MASKED)
        top = jnp.max(scores, -1, keepdims=True)
        weights = jnp.exp(scores - top)
        probs = weights / jnp.sum(weights, -1, keepdims=True)
        probs_low = probs.astype(bf16)
        context = mm(probs_low, v).astype(bf16)
        context_parts.append(context)
        row_delta = jnp.sum(gc.astype(f32) * context.astype(f32), -1, keepdims=True)
        grad_scores = (probs * (mm_t(gc, v) - row_delta) * SCORE_SCALE).astype(bf16)
        grad_q.append(mm(grad_scores, k))
        grad_k.append(t_mm(grad_scores, q))
        grad_v.append(t_mm(probs_low, gc))
    context = pick(jnp.concatenate(context_parts, 1), narrow)
    grad_qkv = jnp.concatenate(
        [
            turn(jnp.concatenate(grad_q, 1), tables, -1.0),
            turn(jnp.concatenate(grad_k, 1), tables, -1.0),
        ]
        + grad_v,
        1,
    ).astype(bf16)

    out_part = mm(context, weight_out) + mlp_out
    grad_attn_in = mm_t(grad_qkv, weight_qkv)

    def pad_wide(value):
        return jnp.pad(value, ((0, 0), (0, width - value.shape[1])))

    natural_vecs = jnp.stack(
        [
            jnp.sum(grad_attn_in * normed, 0),
            jnp.sum(grad_attn_in, 0),
            jnp.sum(grad_mlp_in * normed, 0),
            jnp.sum(grad_mlp_in, 0),
        ]
    ).astype(bf16)
    natural_vecs = mm_t(natural_vecs, wide).astype(bf16)
    bias_grad = jnp.sum(grad_own.astype(f32), 0).astype(bf16)[None]
    bias_up_grad = mm_t(jnp.sum(grad_pre.astype(f32), 0).astype(bf16)[None], hidden_wide).astype(bf16)
    bias_qkv_grad = jnp.sum(grad_qkv.astype(f32), 0).astype(bf16)[None]
    vec_grads = jnp.concatenate(
        [pad_wide(bias_qkv_grad), pad_wide(bias_up_grad), bias_grad, bias_grad, natural_vecs], 0
    )
    vec_rows = sections[2]
    vec_grads = jnp.pad(vec_grads, ((0, dp_count * vec_rows - 8), (0, 0)))
    vec_grads = jnp.transpose(vec_grads.reshape(vec_rows, dp_count, width), (1, 0, 2))
    packed_attn = jnp.concatenate(
        [
            vec_grads,
            parts_of(pad_wide(t_mm(attn_in, grad_qkv).astype(bf16))),
            parts_of(t_mm(context, grad_low).astype(bf16)),
        ],
        1,
    )
    summed_attn = reduce_parts(packed_attn)

    def return_units(summed, low, high):
        total = [0.0, 0.0]
        for j in range(group_count):
            cut = summed[:, j * unit : (j + 1) * unit]
            for half in range(2):
                hot = recv_hot[j, low:high, half * side : (half + 1) * side]
                total[half] = total[half] + t_mm(hot, cut)
        return jnp.concatenate(total, 1)

    vec_own = summed_attn[0].astype(f32)
    matrix_sum = jnp.sum(jnp.square(summed_mlp.astype(f32))) + jnp.sum(
        jnp.square(summed_attn[vec_rows:].astype(f32))
    )
    coarse = lax.reduce_precision(matrix_sum, 8, 7)
    middle = lax.reduce_precision(matrix_sum - coarse, 8, 7)
    fine = lax.reduce_precision(matrix_sum - coarse - middle, 8, 7)
    lane = jnp.arange(2 * unit, dtype=jnp.int32)
    sum_line = jnp.where(
        lane == 0, coarse, jnp.where(lane == 1, middle, jnp.where(lane == 2, fine, 0.0))
    )
    extra = jnp.concatenate([vec_own.reshape(2, 2 * unit), sum_line[None]], 0)
    extra = jnp.pad(extra, ((lines - EXTRA_LINES, 0), (0, 0)))
    returned = return_units(summed_mlp, 0, mlp_rows) + return_units(summed_attn, mlp_rows, total_rows)
    returned = (returned.reshape(-1, lines, 2 * unit) + extra[None]).astype(bf16)
    returned = lax.all_to_all(returned.reshape(-1, 2 * unit), both, 0, 0, tiled=True)
    grad_shard = sum(
        t_mm(send_hot[half], returned[:, half * unit : (half + 1) * unit]) for half in range(2)
    ).reshape(-1)
    extras = returned.reshape(dp_count, group_count, lines, 2 * unit)[:, :, lines - EXTRA_LINES :]
    extras = extras.astype(f32)
    split_sum = jnp.sum(jnp.square(extras[:2, :, :2]))
    shared_sum = jnp.sum(jnp.square(jnp.sum(extras[2:, :, :2], 1)))
    square_sum = jnp.sum(extras[:, :, 2, :3]) + split_sum + shared_sum

    grad_normed = (grad_attn_in * gain_attn + grad_mlp_in * gain_mlp).astype(bf16)
    grad_normed = mm_t(grad_normed, wide).astype(bf16)
    swapped = lax.all_to_all(
        jnp.concatenate([out_part.astype(bf16), grad_normed], 1), "group", 0, 0, tiled=True
    )
    own = jnp.sum(swapped.astype(f32).reshape(group_count, local_rows, 2 * width), 0)
    tokens_own = tokens.astype(f32)
    block_out = (tokens_own + own[:, :width] + bias_rest).astype(bf16)
    own_normed, own_inv = layer_stats(tokens_own)
    grad_in = (grad_own.astype(f32) + norm_backward(own[:, width:], own_normed, own_inv)).astype(bf16)

    return (block_out, grad_in) + update(grad_shard, square_sum, master, moment_one, moment_two)


def pick_t(lhs, rhs):
    return lax.dot_general(
        lhs, rhs, (((1,), (1,)), ((), ())), preferred_element_type=jnp.float32
    ).astype(jnp.bfloat16)


def reduce_parts(packed):
    return lax.psum_scatter(packed, "dp", scatter_dimension=0, tiled=False)


def update(grad_shard, square_sum, master, moment_one, moment_two):
    grad_scale = 1.0 / (jnp.sqrt(square_sum) + 1e-06)
    scaled = grad_shard * grad_scale
    new_one = BETA_ONE * moment_one + (1.0 - BETA_ONE) * scaled
    new_two = BETA_TWO * moment_two + (1.0 - BETA_TWO) * scaled * scaled
    correct_one = 1.0 - BETA_ONE**STEP
    correct_two = 1.0 - BETA_TWO**STEP
    new_master = master - LEARN_RATE * (
        new_one / correct_one / (jnp.sqrt(new_two / correct_two) + ADAM_EPS) + DECAY_RATE * master
    )
    return (grad_shard, new_master, new_one, new_two)


def on_device(tokens, grad_out, segment_ids, positions, counts, master, moment_one, moment_two):
    dp_count, group_count = lax.axis_size("dp"), lax.axis_size("group")
    width = tokens.shape[1]
    splits = (
        (width // HEAD) % group_count == 0
        and FF == width * group_count
        and dp_count >= 8
        and (width // group_count) % dp_count == 0
        and master.shape[0] % (width // group_count) == 0
    )
    body = on_device_split if splits else on_device_gathered
    return body(tokens, grad_out, segment_ids, positions, counts, master, moment_one, moment_two)


def solution(mesh):
    placed = (
        P(("dp", "group"), None),
        P(("dp", "group"), None),
        P(("dp", "group")),
        P(("dp", "group")),
        P(("dp", "group")),
        P(("dp", "group")),
        P(("dp", "group")),
        P(("dp", "group")),
    )
    return jax.shard_map(
        on_device,
        mesh=mesh,
        in_specs=placed,
        out_specs=(
            P(("dp", "group"), None),
            P(("dp", "group"), None),
            P(("dp", "group")),
            P(("dp", "group")),
            P(("dp", "group")),
            P(("dp", "group")),
        ),
        check_vma=False,
    )
```

```python
import functools

import jax
import jax.numpy as jnp
import numpy as np
from jax import lax
from jax.sharding import PartitionSpec as P

FF = 3072
HEAD = 64
ROT = 16
STEP = 3


BETA_ONE = 0.9
BETA_TWO = 0.95
LEARN_RATE = 0.01
DECAY_RATE = 0.1
ADAM_EPS = 1e-08
NORM_EPS = 1e-05
SCORE_SCALE = 0.125
MASKED = -1e30
EXTRA_LINES = 3


def param_layout(model_width, hidden):
    return [
        ("weight_qkv", (model_width, 3 * model_width)),
        ("bias_qkv", (3 * model_width,)),
        ("weight_out", (model_width, model_width)),
        ("bias_out", (model_width,)),
        ("weight_up", (model_width, hidden)),
        ("bias_up", (hidden,)),
        ("weight_down", (hidden, model_width)),
        ("bias_down", (model_width,)),
        ("gain_attn", (model_width,)),
        ("shift_attn", (model_width,)),
        ("gain_mlp", (model_width,)),
        ("shift_mlp", (model_width,)),
    ]


def unpack_params(flat_params, model_width, hidden):
    result = {}
    offset = 0
    for entry_name, entry_shape in param_layout(model_width, hidden):
        length = 1
        for extent in entry_shape:
            length = length * extent
        result[entry_name] = flat_params[offset : offset + length].reshape(entry_shape)
        offset = offset + length
    return result


def pack_grads(grad_dict, model_width, hidden, total_len):
    pieces = []
    used_count = 0
    for entry_name, entry_shape in param_layout(model_width, hidden):
        flat_grad = grad_dict[entry_name].reshape(-1)
        pieces.append(flat_grad)
        used_count = used_count + flat_grad.shape[0]
    pieces.append(jnp.zeros((total_len - used_count,), jnp.float32))
    return jnp.concatenate(pieces)


def rotary_tables(pos_ids):
    half_rot = ROT // 2
    inverse_freq = 10000.0 ** (-jnp.arange(half_rot, dtype=jnp.float32) * 2.0 / ROT)
    angles = pos_ids.astype(jnp.float32)[:, None] * inverse_freq[None, :]
    return (jnp.cos(angles), jnp.sin(angles))


def rotate(values, cosine, sine_rows):
    half_rot = ROT // 2
    lower_part = values[..., :half_rot]
    upper_part = values[..., half_rot:ROT]
    cos_rows = cosine[:, None, :]
    sin_rows = sine_rows[:, None, :]
    return jnp.concatenate(
        [
            lower_part * cos_rows - upper_part * sin_rows,
            upper_part * cos_rows + lower_part * sin_rows,
            values[..., ROT:],
        ],
        -1,
    )


def rotate_back(values, cosine, sine_rows):
    half_rot = ROT // 2
    lower_part = values[..., :half_rot]
    upper_part = values[..., half_rot:ROT]
    cos_rows = cosine[:, None, :]
    sin_rows = sine_rows[:, None, :]
    return jnp.concatenate(
        [
            lower_part * cos_rows + upper_part * sin_rows,
            upper_part * cos_rows - lower_part * sin_rows,
            values[..., ROT:],
        ],
        -1,
    )


def layer_stats(block_in):
    centred = block_in - jnp.mean(block_in, -1, keepdims=True)
    inv_std = lax.rsqrt(jnp.mean(centred * centred, -1, keepdims=True) + NORM_EPS)
    return (centred * inv_std, inv_std)


def norm_backward(grad_normed, normed, inv_std):
    return inv_std * (
        grad_normed
        - jnp.mean(grad_normed, -1, keepdims=True)
        - normed * jnp.mean(grad_normed * normed, -1, keepdims=True)
    )


def gelu_slope(up_pre):
    return (
        0.5 * (1.0 + lax.erf(up_pre * 0.7071067811865476))
        + up_pre * jnp.exp(-0.5 * up_pre * up_pre) * 0.3989422804014327
    )


def masked_scores(query_part, key_part, query_seg, key_seg, query_slot, key_slot):
    scores = (
        jnp.einsum("qhd,khd->hqk", query_part, key_part, preferred_element_type=jnp.float32)
        * SCORE_SCALE
    )
    allowed = (query_seg[:, None] == key_seg[None, :]) & (key_slot[None, :] <= query_slot[:, None])
    return (jnp.where(allowed[None], scores, MASKED), allowed)


def score_grads(scores, allowed, log_total, row_delta, grad_context, value_part):
    attn_probs = jnp.where(allowed[None], jnp.exp(scores - log_total[..., None]), 0.0)
    grad_probs = jnp.einsum(
        "qhd,khd->hqk", grad_context, value_part, preferred_element_type=jnp.float32
    )
    grad_scores = (attn_probs * (grad_probs - row_delta[..., None]) * SCORE_SCALE).astype(
        jnp.bfloat16
    )
    return (attn_probs.astype(jnp.bfloat16), grad_scores)


def on_device_gathered(tokens, grad_out, segment_ids, positions, counts, master, moment_one, moment_two):
    local_rows = tokens.shape[0]
    model_width = tokens.shape[1]
    head_count = model_width // HEAD
    local_master = master.astype(jnp.bfloat16)
    sectioned = lax.all_gather(local_master.reshape(1, 1, -1), "group", axis=1, tiled=True)
    sectioned = lax.all_gather(sectioned, "dp", axis=0, tiled=True)
    flat_params = sectioned.reshape(-1)
    params = unpack_params(flat_params, model_width, FF)
    block_in = tokens.astype(jnp.float32)
    normed, inv_std = layer_stats(block_in)
    gain_attn = params["gain_attn"].astype(jnp.float32)
    gain_mlp = params["gain_mlp"].astype(jnp.float32)
    attn_in = (normed * gain_attn + params["shift_attn"].astype(jnp.float32)).astype(jnp.bfloat16)
    mlp_in = (normed * gain_mlp + params["shift_mlp"].astype(jnp.float32)).astype(jnp.bfloat16)
    qkv_pre = (
        jnp.dot(attn_in, params["weight_qkv"], preferred_element_type=jnp.float32)
        + params["bias_qkv"].astype(jnp.float32)
    ).reshape(local_rows, 3, head_count, HEAD)
    cosine, sine_rows = rotary_tables(positions)
    queries = rotate(qkv_pre[:, 0], cosine, sine_rows).astype(jnp.bfloat16)
    keys_own = rotate(qkv_pre[:, 1], cosine, sine_rows).astype(jnp.bfloat16)
    values_own = qkv_pre[:, 2].astype(jnp.bfloat16)
    key_vals = jnp.stack(
        [keys_own.reshape(local_rows, model_width), values_own.reshape(local_rows, model_width)], 1
    )
    query_slot = lax.axis_index("group") * local_rows + jnp.arange(local_rows, dtype=jnp.int32)

    def split_keys(piece_kv):
        count_keys = piece_kv.shape[0]
        return (
            piece_kv[:, 0].reshape(count_keys, head_count, HEAD),
            piece_kv[:, 1].reshape(count_keys, head_count, HEAD),
        )

    run_max = jnp.full((head_count, local_rows), MASKED, jnp.float32)
    piece_kv = lax.all_gather(key_vals, "group", axis=0, tiled=True)
    piece_seg = lax.all_gather(segment_ids, "group", axis=0, tiled=True)
    piece_keys, piece_values = split_keys(piece_kv)
    key_slot = jnp.arange(piece_seg.shape[0], dtype=jnp.int32)
    scores, allowed = masked_scores(
        queries, piece_keys, segment_ids, piece_seg, query_slot, key_slot
    )
    new_max = jnp.maximum(run_max, jnp.max(scores, -1))
    weights = jnp.where(allowed[None], jnp.exp(scores - new_max[..., None]), 0.0)
    run_sum = jnp.sum(weights, -1)
    run_acc = jnp.einsum(
        "hqk,khd->hqd",
        weights.astype(jnp.bfloat16),
        piece_values,
        preferred_element_type=jnp.float32,
    )
    run_max, run_sum, run_acc = (new_max, run_sum, run_acc)
    log_total = run_max + jnp.log(run_sum)
    context = jnp.transpose(run_acc / run_sum[..., None], (1, 0, 2)).astype(jnp.bfloat16)
    context_flat = context.reshape(local_rows, model_width)
    attn_out = jnp.dot(
        context_flat, params["weight_out"], preferred_element_type=jnp.float32
    ) + params["bias_out"].astype(jnp.float32)
    up_pre = jnp.dot(mlp_in, params["weight_up"], preferred_element_type=jnp.float32) + params[
        "bias_up"
    ].astype(jnp.float32)
    up_act = jax.nn.gelu(up_pre, approximate=False).astype(jnp.bfloat16)
    mlp_out = jnp.dot(up_act, params["weight_down"], preferred_element_type=jnp.float32) + params[
        "bias_down"
    ].astype(jnp.float32)
    block_out = (block_in + attn_out + mlp_out).astype(jnp.bfloat16)
    valid_rows = (jnp.arange(local_rows) < counts[0]).astype(jnp.float32)
    grad_rows = grad_out.astype(jnp.float32) * valid_rows[:, None]
    grad_low = grad_rows.astype(jnp.bfloat16)
    bias_grad = jnp.sum(grad_rows, 0)
    grad_dict = {}
    grad_dict["weight_down"] = jnp.dot(up_act.T, grad_low, preferred_element_type=jnp.float32)
    grad_dict["bias_down"] = bias_grad
    grad_dict["weight_out"] = jnp.dot(context_flat.T, grad_low, preferred_element_type=jnp.float32)
    grad_dict["bias_out"] = bias_grad
    grad_act = jnp.dot(grad_low, params["weight_down"].T, preferred_element_type=jnp.float32)
    grad_pre = (grad_act * gelu_slope(up_pre)).astype(jnp.bfloat16)
    grad_dict["weight_up"] = jnp.dot(mlp_in.T, grad_pre, preferred_element_type=jnp.float32)
    grad_dict["bias_up"] = jnp.sum(grad_pre.astype(jnp.float32), 0)
    grad_mlp_in = jnp.dot(grad_pre, params["weight_up"].T, preferred_element_type=jnp.float32)
    grad_context = jnp.dot(
        grad_low, params["weight_out"].T, preferred_element_type=jnp.float32
    ).astype(jnp.bfloat16)
    grad_context = grad_context.reshape(local_rows, head_count, HEAD)
    row_delta = jnp.einsum(
        "qhd,qhd->hq", grad_context.astype(jnp.float32), context.astype(jnp.float32)
    )
    piece_kv = lax.all_gather(key_vals, "group", axis=0, tiled=True)
    piece_seg = lax.all_gather(segment_ids, "group", axis=0, tiled=True)
    piece_keys, piece_values = split_keys(piece_kv)
    count_keys = piece_seg.shape[0]
    key_slot = jnp.arange(count_keys, dtype=jnp.int32)
    scores, allowed = masked_scores(
        queries, piece_keys, segment_ids, piece_seg, query_slot, key_slot
    )
    probs_low, grad_scores = score_grads(
        scores, allowed, log_total, row_delta, grad_context, piece_values
    )
    grad_queries = jnp.einsum(
        "hqk,khd->qhd", grad_scores, piece_keys, preferred_element_type=jnp.float32
    )
    part_keys = jnp.einsum("hqk,qhd->khd", grad_scores, queries, preferred_element_type=jnp.float32)
    part_values = jnp.einsum(
        "hqk,qhd->khd", probs_low, grad_context, preferred_element_type=jnp.float32
    )
    addition = jnp.stack(
        [part_keys.reshape(count_keys, model_width), part_values.reshape(count_keys, model_width)],
        1,
    )
    grad_kv = addition
    grad_queries, batch_kv = (grad_queries, grad_kv)
    grad_kv = lax.psum_scatter(
        batch_kv.astype(jnp.bfloat16), "group", scatter_dimension=0, tiled=True
    ).astype(jnp.float32)
    grad_keys = grad_kv[:, 0].reshape(local_rows, head_count, HEAD)
    grad_values = grad_kv[:, 1].reshape(local_rows, head_count, HEAD)
    grad_qkv = (
        jnp.stack(
            [
                rotate_back(grad_queries, cosine, sine_rows),
                rotate_back(grad_keys, cosine, sine_rows),
                grad_values,
            ],
            1,
        )
        .reshape(local_rows, 3 * model_width)
        .astype(jnp.bfloat16)
    )
    grad_dict["weight_qkv"] = jnp.dot(attn_in.T, grad_qkv, preferred_element_type=jnp.float32)
    grad_dict["bias_qkv"] = jnp.sum(grad_qkv.astype(jnp.float32), 0)
    grad_attn_in = jnp.dot(grad_qkv, params["weight_qkv"].T, preferred_element_type=jnp.float32)
    grad_dict["gain_attn"] = jnp.sum(grad_attn_in * normed, 0)
    grad_dict["shift_attn"] = jnp.sum(grad_attn_in, 0)
    grad_dict["gain_mlp"] = jnp.sum(grad_mlp_in * normed, 0)
    grad_dict["shift_mlp"] = jnp.sum(grad_mlp_in, 0)
    grad_normed = grad_attn_in * gain_attn + grad_mlp_in * gain_mlp
    grad_in = (grad_rows + norm_backward(grad_normed, normed, inv_std)).astype(jnp.bfloat16)
    dp_count = lax.axis_size("dp")
    group_count = lax.axis_size("group")
    partial_value = pack_grads(grad_dict, model_width, FF, master.shape[0] * dp_count * group_count)
    sectioned_grad = lax.psum_scatter(
        partial_value.reshape(dp_count, group_count, -1).astype(jnp.bfloat16),
        "group",
        scatter_dimension=1,
        tiled=True,
    )
    grad_shard = (
        lax.psum_scatter(sectioned_grad, "dp", scatter_dimension=0, tiled=True)
        .astype(jnp.float32)
        .reshape(-1)
    )
    square_sum = lax.psum(jnp.sum(grad_shard * grad_shard), ("dp", "group"))
    grad_scale = 1.0 / (jnp.sqrt(square_sum) + 1e-06)
    scaled = grad_shard * grad_scale
    new_one = BETA_ONE * moment_one + (1.0 - BETA_ONE) * scaled
    new_two = BETA_TWO * moment_two + (1.0 - BETA_TWO) * scaled * scaled
    correct_one = 1.0 - BETA_ONE**STEP
    correct_two = 1.0 - BETA_TWO**STEP
    new_master = master - LEARN_RATE * (
        new_one / correct_one / (jnp.sqrt(new_two / correct_two) + ADAM_EPS) + DECAY_RATE * master
    )
    return (block_out, grad_in, grad_shard, new_master, new_one, new_two)


def part_rows(model_width, hidden, dp_count, group_count):
    up_rows = model_width // dp_count
    down_rows = hidden // group_count // dp_count
    out_rows = model_width // group_count // dp_count
    vec_rows = -(-8 // dp_count)
    vec_rows = -(-vec_rows // 8) * 8
    return up_rows, down_rows, vec_rows, up_rows, out_rows


@functools.lru_cache(None)
def exchange_tables(model_width, hidden, dp_count, group_count, shard_len):
    width = model_width
    unit = width // group_count
    unit_count = shard_len // unit
    per_line = group_count
    offsets, at = {}, 0
    for entry_name, entry_shape in param_layout(width, hidden):
        offsets[entry_name] = at // width
        at += int(np.prod(entry_shape))
    up_lines = hidden // width
    devices = dp_count * group_count
    sections = part_rows(width, hidden, dp_count, group_count)
    up_rows, down_rows, vec_rows, qkv_rows, out_rows = sections
    total_rows = sum(sections)
    vectors = [
        ("bias_qkv", 3),
        ("bias_up", up_lines),
        ("bias_out", 0),
        ("bias_down", 0),
        ("gain_attn", 0),
        ("shift_attn", 0),
        ("gain_mlp", 0),
        ("shift_mlp", 0),
    ]
    want = np.full((devices, total_rows, per_line), -1, np.int64)
    for d in range(dp_count):
        for g in range(group_count):
            here = want[d * group_count + g]
            row = 0
            for i in range(up_rows):
                r = i * dp_count + d
                for j in range(up_lines):
                    here[row, j] = (offsets["weight_up"] + up_lines * r + j) * per_line + g
                row += 1
            for i in range(down_rows):
                k = i * dp_count + d
                h = width * (k // unit) + unit * g + k % unit
                for j in range(per_line):
                    here[row, j] = (offsets["weight_down"] + h) * per_line + j
                row += 1
            for v, (entry_name, split) in enumerate(vectors):
                if v % dp_count != d:
                    continue
                at_row = row + v // dp_count
                for j in range(split or per_line):
                    base = offsets[entry_name] + (j if split else 0)
                    here[at_row, j] = base * per_line + (g if split else j)
            row += vec_rows
            for i in range(qkv_rows):
                r = i * dp_count + d
                for j in range(3):
                    here[row, j] = (3 * r + j) * per_line + g
                row += 1
            for i in range(out_rows):
                h = unit * g + i * dp_count + d
                for j in range(per_line):
                    here[row, j] = (offsets["weight_out"] + h) * per_line + j
                row += 1
    counts = np.zeros((devices, devices), np.int64)
    sends = [[[] for _ in range(devices)] for _ in range(devices)]
    places = []
    for dest in range(devices):
        for row in range(total_rows):
            for j in range(per_line):
                u = want[dest, row, j]
                if u < 0:
                    continue
                owner = u // unit_count
                slot = counts[owner, dest]
                sends[owner][dest].append(u % unit_count)
                places.append((dest, row, j, owner, slot))
                counts[owner, dest] += 1
    lines = -(-((int(counts.max()) + 1) // 2 + EXTRA_LINES) // 8) * 8
    send = np.full((devices, 2, devices, lines), -1, np.int32)
    for owner in range(devices):
        for dest in range(devices):
            units = sends[owner][dest]
            for slot, u in enumerate(units):
                send[owner, slot % 2, dest, slot // 2] = u
    recv = np.full((devices, per_line, total_rows), -1, np.int32)
    for dest, row, j, owner, slot in places:
        recv[dest, j, row] = (slot % 2 * devices + owner) * lines + slot // 2
    return send.reshape(devices, 2, devices * lines), recv, lines


def spread(size, step):
    each = size // step
    column = np.arange(size)
    natural = (column % each) * step + column // each
    rows = jnp.arange(size, dtype=jnp.int32)
    return (rows[:, None] == jnp.asarray(natural, jnp.int32)[None, :]).astype(jnp.bfloat16)


def pick(lhs, rhs):
    return jnp.dot(lhs, rhs, preferred_element_type=jnp.float32).astype(jnp.bfloat16)


def rotary_wide(pos_ids, width):
    half_rot = ROT // 2
    lane = jnp.arange(width, dtype=jnp.int32) % HEAD
    step = (lane % half_rot).astype(jnp.float32)
    inverse_freq = 10000.0 ** (-step * 2.0 / ROT)
    angles = pos_ids[:, None] * inverse_freq[None, :]
    cosine = jnp.where(lane[None] < ROT, jnp.cos(angles), 1.0)
    sine = jnp.sin(angles)
    low = jnp.where(lane[None] < half_rot, sine, 0.0)
    high = jnp.where((lane[None] >= half_rot) & (lane[None] < ROT), sine, 0.0)
    return cosine, low, high


def turn(values, tables, sign):
    cosine, low, high = tables
    half_rot = ROT // 2
    ahead = jnp.roll(values, -half_rot, 1)
    behind = jnp.roll(values, half_rot, 1)
    return values * cosine + sign * (behind * high - ahead * low)


def on_device_split(tokens, grad_out, segment_ids, positions, counts, master, moment_one, moment_two):
    f32, bf16 = jnp.float32, jnp.bfloat16
    dp_count, group_count = lax.axis_size("dp"), lax.axis_size("group")
    both = ("dp", "group")
    local_rows, width = tokens.shape
    rows = local_rows * group_count
    unit = width // group_count
    hidden = FF // group_count
    heads = unit // HEAD
    shard_len = master.shape[0]
    unit_count = shard_len // unit
    me = lax.axis_index("dp") * group_count + lax.axis_index("group")
    send, recv, lines = exchange_tables(width, FF, dp_count, group_count, shard_len)
    sections = part_rows(width, FF, dp_count, group_count)
    starts = np.cumsum((0,) + sections)
    total_rows = int(starts[-1])
    side = send.shape[2]
    slots = 2 * side
    mlp_rows = int(starts[2])
    first_rows = int(starts[3])

    def mm(lhs, rhs):
        return jnp.dot(lhs, rhs, preferred_element_type=f32)

    def mm_t(lhs, rhs):
        return lax.dot_general(lhs, rhs, (((1,), (1,)), ((), ())), preferred_element_type=f32)

    def t_mm(lhs, rhs):
        return lax.dot_general(lhs, rhs, (((0,), (0,)), ((), ())), preferred_element_type=f32)

    send_row = lax.dynamic_index_in_dim(jnp.asarray(send), me, 0, keepdims=False)
    recv_row = lax.dynamic_index_in_dim(jnp.asarray(recv), me, 0, keepdims=False)
    send_hot = (send_row[:, :, None] == jnp.arange(unit_count, dtype=jnp.int32)).astype(bf16)
    recv_hot = (recv_row[:, :, None] == jnp.arange(slots, dtype=jnp.int32)).astype(bf16)
    back_slots = jnp.arange(slots, dtype=jnp.int32).reshape(2, side, 1)
    back_hot = (recv_row.reshape(1, 1, -1) == back_slots).astype(bf16)
    own_units = master.astype(bf16).reshape(unit_count, unit)
    leaving = jnp.concatenate([pick(send_hot[half], own_units) for half in range(2)], 1)
    moved = lax.all_to_all(leaving, both, 0, 0, tiled=True)
    moved = jnp.concatenate([moved[:, :unit], moved[:, unit:]], 0)

    def gather_rows(low, high):
        count = high - low
        taken = pick(recv_hot[:, low:high].reshape(-1, slots), moved)
        taken = [taken[j * count : (j + 1) * count] for j in range(group_count)]
        return lax.all_gather(jnp.concatenate(taken, 1), "dp", axis=0, tiled=False)

    whole_mlp = gather_rows(0, first_rows)
    whole_attn = gather_rows(first_rows, total_rows)
    weight_up = whole_mlp[:, : starts[1]].reshape(-1, width)
    weight_down = whole_mlp[:, starts[1] : mlp_rows].reshape(-1, width)
    vec_all = whole_mlp[:8, mlp_rows]
    wide = spread(width, dp_count)
    narrow = spread(unit, dp_count)
    hidden_wide = spread(hidden, dp_count)
    bias_qkv = vec_all[0].astype(f32)[: 3 * unit]
    weight_up = pick(weight_up, hidden_wide)
    vec_turned = pick(vec_all, wide).astype(f32)
    bias_up = pick(vec_all[1:2, :hidden], hidden_wide).astype(f32)[0]
    bias_rest = vec_all[2].astype(f32) + vec_all[3].astype(f32)
    gain_attn, shift_attn, gain_mlp, shift_mlp = (vec_turned[4 + i] for i in range(4))

    valid_rows = jnp.arange(local_rows) < counts[0]
    grad_own = jnp.where(valid_rows[:, None], grad_out, jnp.zeros_like(grad_out))
    base = 256
    digits = [segment_ids // base, segment_ids % base, positions // base, positions % base]
    digits = jnp.stack(digits, 1).astype(bf16)
    digits = jnp.pad(digits, ((0, 0), (0, 124)))
    batch = lax.all_gather(
        jnp.concatenate([tokens, grad_own, digits], 1), "group", axis=0, tiled=True
    )
    grad_low = batch[:, width : 2 * width]
    digits = batch[:, 2 * width :].astype(f32)
    segment = digits[:, 0] * base + digits[:, 1]
    place = digits[:, 2] * base + digits[:, 3]
    block_in = mm(batch[:, :width], wide)
    normed, inv_std = layer_stats(block_in)
    attn_in = (normed * gain_attn + shift_attn).astype(bf16)
    mlp_in = (normed * gain_mlp + shift_mlp).astype(bf16)

    def parts_of(value):
        return value.reshape(dp_count, -1, width)

    up_pre = mm(mlp_in, weight_up) + bias_up
    up_act = jax.nn.gelu(up_pre, approximate=False).astype(bf16)
    mlp_out = mm(up_act, weight_down)
    grad_pre = (mm_t(grad_low, weight_down) * gelu_slope(up_pre)).astype(bf16)
    grad_mlp_in = mm_t(grad_pre, weight_up)
    packed_mlp = jnp.concatenate(
        [
            parts_of(mm_t(t_mm(mlp_in, grad_pre).astype(bf16), hidden_wide).astype(bf16)),
            parts_of(t_mm(up_act, grad_low).astype(bf16)),
        ],
        1,
    )
    whole_attn, packed_mlp = lax.optimization_barrier((whole_attn, packed_mlp))
    summed_mlp = reduce_parts(packed_mlp)
    weight_qkv = whole_attn[:, : sections[3]].reshape(-1, width)[:, : 3 * unit]
    weight_out = whole_attn[:, sections[3] :].reshape(-1, width)

    qkv_pre = mm(attn_in, weight_qkv) + bias_qkv
    tables = rotary_wide(place, unit)
    queries = turn(qkv_pre[:, :unit], tables, 1.0).astype(bf16)
    keys = turn(qkv_pre[:, unit : 2 * unit], tables, 1.0).astype(bf16)
    values = qkv_pre[:, 2 * unit :].astype(bf16)
    slot = jnp.arange(rows, dtype=jnp.int32)
    allowed = (segment[:, None] == segment[None, :]) & (slot[None, :] <= slot[:, None])

    grad_context = pick_t(grad_low, weight_out)
    grad_context = mm_t(grad_context, narrow).astype(bf16)
    context_parts, grad_q, grad_k, grad_v = [], [], [], []
    for h in range(heads):
        cut = slice(h * HEAD, (h + 1) * HEAD)
        q, k, v, gc = queries[:, cut], keys[:, cut], values[:, cut], grad_context[:, cut]
        scores = jnp.where(allowed, mm_t(q, k) * SCORE_SCALE, MASKED)
        top = jnp.max(scores, -1, keepdims=True)
        weights = jnp.exp(scores - top)
        probs = weights / jnp.sum(weights, -1, keepdims=True)
        probs_low = probs.astype(bf16)
        context = mm(probs_low, v).astype(bf16)
        context_parts.append(context)
        row_delta = jnp.sum(gc.astype(f32) * context.astype(f32), -1, keepdims=True)
        grad_scores = (probs * (mm_t(gc, v) - row_delta) * SCORE_SCALE).astype(bf16)
        grad_q.append(mm(grad_scores, k))
        grad_k.append(t_mm(grad_scores, q))
        grad_v.append(t_mm(probs_low, gc))
    context = pick(jnp.concatenate(context_parts, 1), narrow)
    grad_qkv = jnp.concatenate(
        [
            turn(jnp.concatenate(grad_q, 1), tables, -1.0),
            turn(jnp.concatenate(grad_k, 1), tables, -1.0),
        ]
        + grad_v,
        1,
    ).astype(bf16)

    out_part = mm(context, weight_out) + mlp_out
    grad_attn_in = mm_t(grad_qkv, weight_qkv)

    def pad_wide(value):
        return jnp.pad(value, ((0, 0), (0, width - value.shape[1])))

    natural_vecs = jnp.stack(
        [
            jnp.sum(grad_attn_in * normed, 0),
            jnp.sum(grad_attn_in, 0),
            jnp.sum(grad_mlp_in * normed, 0),
            jnp.sum(grad_mlp_in, 0),
        ]
    ).astype(bf16)
    natural_vecs = mm_t(natural_vecs, wide).astype(bf16)
    bias_grad = jnp.sum(grad_own.astype(f32), 0).astype(bf16)[None]
    bias_up_grad = mm_t(jnp.sum(grad_pre.astype(f32), 0).astype(bf16)[None], hidden_wide).astype(bf16)
    bias_qkv_grad = jnp.sum(grad_qkv.astype(f32), 0).astype(bf16)[None]
    vec_grads = jnp.concatenate(
        [pad_wide(bias_qkv_grad), pad_wide(bias_up_grad), bias_grad, bias_grad, natural_vecs], 0
    )
    vec_rows = sections[2]
    vec_grads = jnp.pad(vec_grads, ((0, dp_count * vec_rows - 8), (0, 0)))
    vec_grads = jnp.transpose(vec_grads.reshape(vec_rows, dp_count, width), (1, 0, 2))
    packed_attn = jnp.concatenate(
        [
            vec_grads,
            parts_of(pad_wide(t_mm(attn_in, grad_qkv).astype(bf16))),
            parts_of(t_mm(context, grad_low).astype(bf16)),
        ],
        1,
    )
    packed_attn, summed_mlp = lax.optimization_barrier((packed_attn, summed_mlp))
    summed_attn = reduce_parts(packed_attn)

    vec_own = summed_attn[0].astype(f32)
    matrix_sum = jnp.sum(jnp.square(summed_mlp.astype(f32))) + jnp.sum(
        jnp.square(summed_attn[vec_rows:].astype(f32))
    )
    coarse = lax.reduce_precision(matrix_sum, 8, 7)
    middle = lax.reduce_precision(matrix_sum - coarse, 8, 7)
    fine = lax.reduce_precision(matrix_sum - coarse - middle, 8, 7)
    lane = jnp.arange(2 * unit, dtype=jnp.int32)
    sum_line = jnp.where(
        lane == 0, coarse, jnp.where(lane == 1, middle, jnp.where(lane == 2, fine, 0.0))
    )
    extra = jnp.concatenate([vec_own.reshape(2, 2 * unit), sum_line[None]], 0)
    extra = jnp.pad(extra, ((lines - EXTRA_LINES, 0), (0, 0)))
    summed = jnp.concatenate([summed_mlp, summed_attn], 0)
    units = jnp.concatenate(
        [summed[:, j * unit : (j + 1) * unit] for j in range(group_count)], 0
    )
    returned = jnp.concatenate([pick(back_hot[half], units) for half in range(2)], 1)
    returned = returned.reshape(-1, lines, 2 * unit) + extra.astype(bf16)[None]
    returned = lax.all_to_all(returned.reshape(-1, 2 * unit), both, 0, 0, tiled=True)
    grad_shard = sum(
        t_mm(send_hot[half], returned[:, half * unit : (half + 1) * unit]) for half in range(2)
    ).reshape(-1)
    extras = returned.reshape(dp_count, group_count, lines, 2 * unit)[:, :, lines - EXTRA_LINES :]
    extras = extras.astype(f32)
    split_sum = jnp.sum(jnp.square(extras[:2, :, :2]))
    shared_sum = jnp.sum(jnp.square(jnp.sum(extras[2:, :, :2], 1)))
    square_sum = jnp.sum(extras[:, :, 2, :3]) + split_sum + shared_sum

    grad_normed = (grad_attn_in * gain_attn + grad_mlp_in * gain_mlp).astype(bf16)
    grad_normed = mm_t(grad_normed, wide).astype(bf16)
    swapped = lax.all_to_all(
        jnp.concatenate([out_part.astype(bf16), grad_normed], 1), "group", 0, 0, tiled=True
    )
    own = jnp.sum(swapped.astype(f32).reshape(group_count, local_rows, 2 * width), 0)
    tokens_own = tokens.astype(f32)
    block_out = (tokens_own + own[:, :width] + bias_rest).astype(bf16)
    own_normed, own_inv = layer_stats(tokens_own)
    grad_in = (grad_own.astype(f32) + norm_backward(own[:, width:], own_normed, own_inv)).astype(bf16)

    return (block_out, grad_in) + update(grad_shard, square_sum, master, moment_one, moment_two)


def pick_t(lhs, rhs):
    return lax.dot_general(
        lhs, rhs, (((1,), (1,)), ((), ())), preferred_element_type=jnp.float32
    ).astype(jnp.bfloat16)


def reduce_parts(packed):
    return lax.psum_scatter(packed, "dp", scatter_dimension=0, tiled=False)


def update(grad_shard, square_sum, master, moment_one, moment_two):
    grad_scale = 1.0 / (jnp.sqrt(square_sum) + 1e-06)
    scaled = grad_shard * grad_scale
    new_one = BETA_ONE * moment_one + (1.0 - BETA_ONE) * scaled
    new_two = BETA_TWO * moment_two + (1.0 - BETA_TWO) * scaled * scaled
    correct_one = 1.0 - BETA_ONE**STEP
    correct_two = 1.0 - BETA_TWO**STEP
    new_master = master - LEARN_RATE * (
        new_one / correct_one / (jnp.sqrt(new_two / correct_two) + ADAM_EPS) + DECAY_RATE * master
    )
    return (grad_shard, new_master, new_one, new_two)


def on_device(tokens, grad_out, segment_ids, positions, counts, master, moment_one, moment_two):
    dp_count, group_count = lax.axis_size("dp"), lax.axis_size("group")
    width = tokens.shape[1]
    splits = (
        (width // HEAD) % group_count == 0
        and FF == width * group_count
        and dp_count >= 8
        and (width // group_count) % dp_count == 0
        and master.shape[0] % (width // group_count) == 0
    )
    body = on_device_split if splits else on_device_gathered
    return body(tokens, grad_out, segment_ids, positions, counts, master, moment_one, moment_two)


def solution(mesh):
    placed = (
        P(("dp", "group"), None),
        P(("dp", "group"), None),
        P(("dp", "group")),
        P(("dp", "group")),
        P(("dp", "group")),
        P(("dp", "group")),
        P(("dp", "group")),
        P(("dp", "group")),
    )
    return jax.shard_map(
        on_device,
        mesh=mesh,
        in_specs=placed,
        out_specs=(
            P(("dp", "group"), None),
            P(("dp", "group"), None),
            P(("dp", "group")),
            P(("dp", "group")),
            P(("dp", "group")),
            P(("dp", "group")),
        ),
        check_vma=False,
    )
```
